32 devices in a mesh: slab: 4 (over y, core), tile: 8 (over z, x).
Axes of the slice: x: 2, y: 2, z: 4, core: 2. Of those that a mesh axis runs over, the one named last changes fastest.
Arguments:
- electric: float32 [3, 56, 256, 1024], P(None, 'slab', 'tile'), may hold values from -6 to 6
- current: float32 [3, 56, 256, 1024], P(None, 'slab', 'tile'), may hold values from -6 to 6
- mass_shift: float32 [56, 256, 1024], P('slab', 'tile'), may hold values from 0.5 to 4
- interface: float32 [4, 2, 2, 256, 1024], P('slab', None, None, 'tile'), may hold values from -6 to 6
- auxiliary: float32 [4, 2, 4, 2, 256, 1024], P('slab', None, None, None, 'tile'), may hold values from -3 to 3
Outputs:
- smoothed: float32 [3, 56, 256, 1024], P(None, 'slab', 'tile')
- next_interface: float32 [4, 2, 2, 256, 1024], P('slab', None, None, 'tile')
- next_auxiliary: float32 [4, 2, 4, 2, 256, 1024], P('slab', None, None, None, 'tile')
The draws below stay inside these ranges and needn't reach their ends.
All inputs are finite; a program needn't handle non-finite values.
Results may differ from the reference program's by a relative error of at most 0.0001.
Values sent between devices are 32-bit elements; how exact they have to be, the bound alone decides.
No kernel may reach another device: no remote copies, remote signals or barrier semaphores. Data moves between devices by JAX's collectives and lax.ppermute only.
A program may use at most 128 MiB of HBM per device.

```python
import math
import jax
import jax.numpy as jnp
from jax import lax

X = 1024
PZ = 14
SLABS = 4
NY = 256
NZ = 56


def shard_levels(rng, dims, pieces, smallest, largest):
    def one(dim, parts):
        draws = jax.random.uniform(jax.random.fold_in(jax.random.fold_in(rng, 6), dim), (parts,), jnp.float32, smallest / len(pieces), largest / len(pieces))
        return jnp.repeat(jnp.exp(draws), dims[dim] // parts).reshape((-1,) + (1,) * (len(dims) - dim - 1))

    level = one(*pieces[0])
    for cut in pieces[1:]:
        level = level * one(*cut)
    return level


def normal_values(rng, extent, spread, reach, shards=(), dtype=jnp.bfloat16):
    factor_of = shard_levels(rng, extent, shards, -0.22, 0.18) if shards else 1.0
    result = jax.random.normal(rng, extent, jnp.float32) * spread * factor_of
    return jnp.minimum(jnp.maximum(result, -reach), reach).astype(dtype)


def setup_inputs(seed: int = 0) -> dict:
    splits = jax.random.split(jax.random.key(seed), 6)
    return {
        "electric": normal_values(splits[0], (3, NZ, NY, X), 1.0, 6.0, ((1, 4), (2, 8)), jnp.float32),
        "current": normal_values(splits[1], (3, NZ, NY, X), 1.0, 6.0, ((1, 4), (2, 8)), jnp.float32),
        "mass_shift": jnp.clip(jnp.exp(math.log(4.0) - 2.0794415 * jax.random.uniform(splits[2], (NZ, NY, X), jnp.float32) ** shard_levels(splits[2], (NZ, NY, X), ((0, 4), (1, 8)), -0.2, 0.2)), 0.5, 4.0),
        "interface": normal_values(splits[3], (SLABS, 2, 2, NY, X), 1.0, 6.0, ((0, 4), (3, 8)), jnp.float32),
        "auxiliary": normal_values(splits[4], (SLABS, 2, 4, 2, NY, X), 0.5, 3.0, ((0, 4), (4, 8)), jnp.float32),
    }


pade_weights = [2.0 / 9.0 * math.sin(j * math.pi / 9.0) ** 2 for j in range(1, 5)]
pade_decays = [math.cos(j * math.pi / 9.0) ** 2 for j in range(1, 5)]


def forward_diff(values, along):
    along = along % values.ndim
    count = values.shape[along]
    shifted = jnp.concatenate([lax.slice_in_dim(values, 1, count, axis=along), jnp.zeros_like(lax.slice_in_dim(values, 0, 1, axis=along))], along)
    return shifted - values


def backward_diff(values, along):
    along = along % values.ndim
    count = values.shape[along]
    shifted = jnp.concatenate([jnp.zeros_like(lax.slice_in_dim(values, 0, 1, axis=along)), lax.slice_in_dim(values, 0, count - 1, axis=along)], along)
    return values - shifted


def curl_curl(padded):
    field_x, field_y, field_z = padded[0], padded[1], padded[2]
    flux_x = forward_diff(field_z, 1) - forward_diff(field_y, 0)
    flux_y = forward_diff(field_x, 0) - forward_diff(field_z, 2)
    flux_z = forward_diff(field_y, 2) - forward_diff(field_x, 1)
    image_x = backward_diff(flux_z, 1) - backward_diff(flux_y, 0)
    image_y = backward_diff(flux_x, 0) - backward_diff(flux_z, 2)
    image_z = backward_diff(flux_y, 2) - backward_diff(flux_x, 1)
    return jnp.stack([image_x, image_y, image_z])[:, 1:-1, 1:-1, :]


def update(padded, current, mass_shift):
    interior = padded[:, 1:-1, 1:-1, :]
    residual = current - (curl_curl(padded) + mass_shift * interior)
    return interior + 0.5 * residual / (mass_shift + 4.0)


def surface(padded):
    comp_x = padded[..., 0, :, :]
    comp_y = padded[..., 1, :, :]
    divergence = backward_diff(comp_x, -1) + backward_diff(comp_y, -2)
    rotation = forward_diff(comp_y, -1) - forward_diff(comp_x, -2)
    vort_x = backward_diff(rotation, -2) - forward_diff(divergence, -1)
    vort_y = -backward_diff(rotation, -1) - forward_diff(divergence, -2)
    return (jnp.stack([vort_x, vort_y], axis=-3) / 8.0)[..., 1:-1, :]


def reference(electric, current, mass_shift, interface, auxiliary):
    weights = jnp.asarray(pade_weights, jnp.float32).reshape(1, 4, 1, 1, 1)
    decays = jnp.asarray(pade_decays, jnp.float32).reshape(1, 4, 1, 1, 1)
    fields = []
    outgoing_all = []
    auxiliary_all = []
    for slab_index in range(SLABS):
        planes = slice(slab_index * PZ, (slab_index + 1) * PZ)
        local_field = electric[:, planes]
        local_current = current[:, planes]
        local_shift = mass_shift[planes]
        zero_plane = jnp.zeros((1, NY, X), jnp.float32)
        below_ghost = jnp.concatenate([interface[slab_index, 0], zero_plane], 0)
        above_ghost = jnp.concatenate([interface[slab_index, 1], zero_plane], 0)
        for sweep_index in range(2):
            extended = jnp.concatenate([below_ghost[:, None], local_field, above_ghost[:, None]], 1)
            padded = jnp.pad(extended, ((0, 0), (0, 0), (1, 1), (0, 0)))
            local_field = update(padded, local_current, local_shift)
        fields.append(local_field)
        traces = jnp.stack([local_field[0:2, 0], local_field[0:2, -1]])
        combined = traces[:, None] - decays * auxiliary[slab_index]
        padded_surface = jnp.pad(combined, ((0, 0), (0, 0), (0, 0), (1, 1), (0, 0)))
        new_auxiliary = surface(padded_surface)
        auxiliary_all.append(new_auxiliary)
        outgoing_all.append(traces + jnp.sum(weights * new_auxiliary, axis=1))
    zero_face = jnp.zeros((2, NY, X), jnp.float32)
    interfaces = []
    for slab_index in range(SLABS):
        from_below = outgoing_all[slab_index - 1][1] if slab_index > 0 else zero_face
        from_above = outgoing_all[slab_index + 1][0] if slab_index < SLABS - 1 else zero_face
        interfaces.append(jnp.stack([from_below, from_above]))
    return jnp.concatenate(fields, axis=1), jnp.stack(interfaces), jnp.stack(auxiliary_all)
```

```python
import functools
import math

import jax
import jax.numpy as jnp
from jax import lax
from jax.experimental import pallas as pl
from jax.experimental.pallas import tpu as pltpu
from jax.sharding import PartitionSpec as P

pade_weights = [2.0 / 9.0 * math.sin(j * math.pi / 9.0) ** 2 for j in range(1, 5)]
pade_decays = [math.cos(j * math.pi / 9.0) ** 2 for j in range(1, 5)]
TERMS = 4
SUB, LANE = 8, 128
F32 = jnp.float32
HBM = pl.BlockSpec(memory_space=pltpu.HBM)
VM = pl.BlockSpec(memory_space=pltpu.VMEM)


def params(mib):
    return pltpu.CompilerParams(vmem_limit_bytes=mib << 20)


def shape(*dims):
    return jax.ShapeDtypeStruct(dims, F32)


def cost(flops, count):
    return pl.CostEstimate(flops=flops, bytes_accessed=count, transcendentals=0)


def vm(*dims):
    return pltpu.VMEM(dims, F32)


def row_next(row):
    n = row.shape[1]
    at = lax.broadcasted_iota(jnp.int32, row.shape, 1)
    return jnp.where(at == n - 1, 0.0, pltpu.roll(row, n - 1, 1))


def row_prev(row):
    at = lax.broadcasted_iota(jnp.int32, row.shape, 1)
    return jnp.where(at == 0, 0.0, pltpu.roll(row, 1, 1))


def pack_rows(nz, first, last, top_y, send_up, send_down):
    here = last(0)
    for z in range(nz):
        low_x, low_z = first(z)
        send_down[z, 0:1, :] = low_x
        send_down[z, 1:2, :] = low_z
        x, y, zc = here
        here = last(z + 1) if z + 1 < nz else None
        y_above = top_y() if here is None else here[1]
        send_up[z, 0:1, :] = row_next(y) - y + x
        send_up[z, 1:2, :] = zc + (y_above - y)


def fixed_first(field, weight, low, z):
    w = weight[z, 0:1, :]
    return field[0, z, 0:1, :] + w * low[z, 0:1, :], field[2, z, 0:1, :] + w * low[z, 1:2, :]


def fixed_last(field, weight, high, z, ny):
    end = slice(ny - 1, ny)
    w = weight[z, end, :]
    hx, hz = high[z, 0:1, :], high[z, 1:2, :]
    rise = hz - high[z - 1, 1:2, :] if z else hz
    return (
        field[0, z, end, :] + w * hx,
        field[1, z, end, :] - w * (rise + (hx - row_prev(hx))),
        field[2, z, end, :] + w * hz,
    )


def lane_masks():
    lane = lax.broadcasted_iota(jnp.int32, (SUB, LANE), 1)
    sub = lax.broadcasted_iota(jnp.int32, (SUB, LANE), 0)
    return lane == 0, lane == LANE - 1, sub == 0, sub == SUB - 1


def tile_at(i, c):
    return slice(i * SUB, (i + 1) * SUB), slice(c * LANE, (c + 1) * LANE)


def pack_kernel(dims, electric, faces, send_up, send_down, first, last, top, sem):
    nz, ny, nx = dims
    copies = [
        pltpu.make_async_copy(electric.at[:, :, pl.ds(ny - SUB, SUB)], last, sem.at[0]),
        pltpu.make_async_copy(electric.at[:, :, pl.ds(0, SUB)], first, sem.at[1]),
        pltpu.make_async_copy(faces.at[0, 1, 1, pl.ds(ny - SUB, SUB)], top, sem.at[2]),
    ]
    for copy in copies:
        copy.start()
    for copy in copies:
        copy.wait()
    pack_rows(
        nz,
        lambda z: (first[0, z, 0:1, :], first[2, z, 0:1, :]),
        lambda z: tuple(last[k, z, SUB - 1 : SUB, :] for k in range(3)),
        lambda: top[SUB - 1 : SUB, :],
        send_up,
        send_down,
    )


def sweep_planes(load, store, current, weight, ghost, hx_s, hy_s, dims, before_plane, from_mass):
    nz, ny, nx = dims
    rows, cols = ny // SUB, nx // LANE
    is_first_lane, is_last_lane, is_first_sub, is_last_sub = lane_masks()

    for i in range(rows):
        for c in range(cols):
            r, s = tile_at(i, c)
            hx_s[r, s] = ghost[1, r, s] - load(1, 0, i, c)
            hy_s[r, s] = load(0, 0, i, c) - ghost[0, r, s]

    def plane(z, carry):
        before_plane(z)

        def left(k, i, c):
            return pltpu.roll(load(k, z, i, c), LANE - 1, 1)

        lefts = {(k, i): left(k, i, 0) for k in (1, 2) for i in range(rows)}
        right_y, right_z = {}, {}
        for c in range(cols):
            here = [[load(k, z, i, c) for k in range(3)] for i in range(rows)]
            ups = [{k: pltpu.roll(here[i][k], SUB - 1, 0) for k in (0, 2)} for i in range(rows)]
            down_x = down_z = None
            for i in range(rows):
                r, s = tile_at(i, c)

                def y_next(k):
                    return jnp.where(is_last_sub, ups[i + 1][k] if i + 1 < rows else 0.0, ups[i][k])

                def x_next(k):
                    after = left(k, i, c + 1) if c + 1 < cols else 0.0
                    value = jnp.where(is_last_lane, after, lefts[k, i])
                    lefts[k, i] = after
                    return value

                ex, ey, ez = here[i]
                hx = (y_next(2) - ez) - (load(1, z + 1, i, c) - ey)
                hy = (load(0, z + 1, i, c) - ex) - (x_next(2) - ez)
                hz = (x_next(1) - ey) - (y_next(0) - ex)
                hx_low, hy_low = hx_s[r, s], hy_s[r, s]
                hx_s[r, s] = hx
                hy_s[r, s] = hy
                dx = pltpu.roll(hx, 1, 0)
                dz = pltpu.roll(hz, 1, 0)
                hx_y = jnp.where(is_first_sub, ez if i == 0 else down_x, dx)
                hz_y = jnp.where(is_first_sub, -ex if i == 0 else down_z, dz)
                down_x, down_z = dx, dz
                ry = pltpu.roll(hy, 1, 1)
                rz = pltpu.roll(hz, 1, 1)
                hy_x = jnp.where(is_first_lane, 0.0 if c == 0 else right_y[i], ry)
                hz_x = jnp.where(is_first_lane, 0.0 if c == 0 else right_z[i], rz)
                right_y[i], right_z[i] = ry, rz
                cx = (hz - hz_y) - (hy - hy_low)
                cy = (hx - hx_low) - (hz - hz_x)
                cz = (hy - hy_x) - (hx - hx_y)
                w = weight[z, r, s]
                if from_mass:
                    w = 0.5 / (w + 4.0)
                    weight[z, r, s] = w
                keep = 4.0 * w + 0.5
                store(0, z, i, c, keep * ex + w * (current[0, z, r, s] - cx))
                store(1, z, i, c, keep * ey + w * (current[1, z, r, s] - cy))
                store(2, z, i, c, keep * ez + w * (current[2, z, r, s] - cz))
        return carry

    lax.fori_loop(0, nz, plane, 0)


def first_kernel(
    dims, electric, current_h, mass, faces, aux_h,
    field, current, weight, ghost, aux, hx_s, hy_s, field_sem, current_sem, weight_sem, face_sem,
):
    nz, ny, nx = dims
    copy = pltpu.make_async_copy

    def field_copy(z):
        return copy(electric.at[:, pl.ds(z, 1)], field.at[:, pl.ds(z, 1)], field_sem.at[z])

    def current_copy(z):
        return copy(current_h.at[:, pl.ds(z, 1)], current.at[:, pl.ds(z, 1)], current_sem.at[z])

    def weight_copy(z):
        return copy(mass.at[pl.ds(z, 1)], weight.at[pl.ds(z, 1)], weight_sem.at[z])

    low_copy = copy(faces.at[0, 0], ghost, face_sem.at[0])
    high_copies = [copy(faces.at[0, 1, k], field.at[k, nz], face_sem.at[1 + k]) for k in range(2)]
    aux_copy = copy(aux_h.at[0], aux, face_sem.at[3])
    low_copy.start()
    field_copy(0).start()

    def start(z, carry):
        field_copy(z + 1).start()
        current_copy(z).start()
        weight_copy(z).start()
        return carry

    lax.fori_loop(0, nz - 1, start, 0)
    current_copy(nz - 1).start()
    weight_copy(nz - 1).start()
    for high in high_copies:
        high.start()
    aux_copy.start()

    def before_plane(z):
        @pl.when(z + 1 < nz)
        def _():
            field_copy(z + 1).wait()

        @pl.when(z + 1 == nz)
        def _():
            for high in high_copies:
                high.wait()

        current_copy(z).wait()
        weight_copy(z).wait()

    def load(k, z, i, c):
        r, s = tile_at(i, c)
        return field[k, z, r, s]

    def store(k, z, i, c, value):
        r, s = tile_at(i, c)
        field[k, z, r, s] = value

    low_copy.wait()
    field_copy(0).wait()
    sweep_planes(load, store, current, weight, ghost, hx_s, hy_s, dims, before_plane, True)
    aux_copy.wait()


def fix_pack_kernel(dims, field, weight, low, high, head, tail, send_up, send_down):
    nz, ny, nx = dims
    for z in range(nz):
        head[z, 0:1, :], head[z, 1:2, :] = fixed_first(field, weight, low, z)
        x, y, zc = fixed_last(field, weight, high, z, ny)
        tail[z, 0:1, :], tail[z, 1:2, :], tail[z, 2:3, :] = x, y, zc
    end = slice(ny - 1, ny)
    head[nz, 0:1, :] = field[0, nz, 0:1, :]
    tail[nz, 0:1, :] = field[0, nz, end, :]
    tail[nz, 1:2, :] = field[1, nz, end, :]
    pack_rows(
        nz,
        lambda z: (head[z, 0:1, :], head[z, 1:2, :]),
        lambda z: tuple(tail[z, k : k + 1, :] for k in range(3)),
        lambda: tail[nz, 1:2, :],
        send_up,
        send_down,
    )


def second_kernel(dims, old, current, weight, ghost, head, tail, field, hx_s, hy_s):
    nz, ny, nx = dims
    rows = ny // SUB
    _, _, is_first_sub, is_last_sub = lane_masks()

    def load(k, z, i, c):
        r, s = tile_at(i, c)
        value = old[k, z, r, s]
        if i == 0 and k != 1:
            value = jnp.where(is_first_sub, head[z, k // 2 : k // 2 + 1, s], value)
        if i == rows - 1:
            value = jnp.where(is_last_sub, tail[z, k : k + 1, s], value)
        return value

    def store(k, z, i, c, value):
        r, s = tile_at(i, c)
        field[k, z, r, s] = value

    sweep_planes(load, store, current, weight, ghost, hx_s, hy_s, dims, lambda z: None, False)


def fix_trace_kernel(dims, field, weight, aux, low, high, head, tail, traces, send_up, send_down):
    nz, ny, nx = dims
    end = slice(ny - 1, ny)
    for side in range(2):
        z = (nz - 1) * side
        for k in range(2):
            traces[side, k] = field[k, z]
    for z in range(nz):
        head[z, 0:1, :], head[z, 1:2, :] = fixed_first(field, weight, low, z)
        x, y, zc = fixed_last(field, weight, high, z, ny)
        tail[z, 0:1, :], tail[z, 1:2, :], tail[z, 2:3, :] = x, y, zc
        if z in (0, nz - 1):
            side = 0 if z == 0 else 1
            traces[side, 0, 0:1, :] = head[z, 0:1, :]
            traces[side, 0, end, :] = x
            traces[side, 1, end, :] = y
    for side in range(2):
        for k in range(2):
            first = traces[side, k, 0:1, :]
            last = traces[side, k, end, :]
            for j in range(TERMS):
                at = side * TERMS + j
                send_down[at, k : k + 1, :] = first - pade_decays[j] * aux[side, j, k, 0:1, :]
                send_up[at, k : k + 1, :] = last - pade_decays[j] * aux[side, j, k, end, :]


def surface_kernel(dims, field, head, tail, traces, aux, smoothed, fresh, outgoing, edges, sem):
    nz, ny, nx = dims
    rows, cols = ny // SUB, nx // LANE
    is_first_lane, is_last_lane, is_first_sub, is_last_sub = lane_masks()
    spans = [(0, SUB), (ny - SUB, SUB)]
    middle = pltpu.make_async_copy(
        field.at[:, pl.ds(0, nz), pl.ds(SUB, ny - 2 * SUB)], smoothed.at[:, :, pl.ds(SUB, ny - 2 * SUB)], sem.at[0]
    )
    middle.start()

    def merge(z, carry):
        for c in range(cols):
            s = slice(c * LANE, (c + 1) * LANE)
            for k in range(3):
                value = field[k, z, 0:SUB, s]
                if k != 1:
                    value = jnp.where(is_first_sub, head[z, k // 2 : k // 2 + 1, s], value)
                edges[0, k, z, :, s] = value
                value = field[k, z, ny - SUB : ny, s]
                edges[1, k, z, :, s] = jnp.where(is_last_sub, tail[z, k : k + 1, s], value)
        return carry

    lax.fori_loop(0, nz, merge, 0)
    outer = [
        pltpu.make_async_copy(edges.at[e], smoothed.at[:, :, pl.ds(*spans[e])], sem.at[1 + e]) for e in range(2)
    ]
    for copy in outer:
        copy.start()

    def part(side, carry):
        outgoing[side] = traces[side]

        def term(j, carry):
            decay = weight = F32(0.0)
            for q in range(TERMS):
                decay = jnp.where(j == q, F32(pade_decays[q]), decay)
                weight = jnp.where(j == q, F32(pade_weights[q]), weight)
            for k in range(2):

                def value(i, c):
                    r, s = tile_at(i, c)
                    return traces[side, k, r, s] - decay * aux[side, j, k, r, s]

                column = [value(i, 0) for i in range(rows)]
                lefts = [pltpu.roll(u, LANE - 1, 1) for u in column]
                rights = [0.0] * rows
                for c in range(cols):
                    ups = [pltpu.roll(u, SUB - 1, 0) for u in column]
                    downs = [pltpu.roll(u, 1, 0) for u in column]
                    after = [value(i, c + 1) for i in range(rows)] if c + 1 < cols else None
                    for i in range(rows):
                        r, s = tile_at(i, c)
                        u = column[i]
                        y_next = jnp.where(is_last_sub, ups[i + 1] if i + 1 < rows else 0.0, ups[i])
                        y_prev = jnp.where(is_first_sub, downs[i - 1] if i else 0.0, downs[i])
                        if after is not None:
                            beyond = pltpu.roll(after[i], LANE - 1, 1)
                        else:
                            beyond = u if k == 0 else 0.0
                        x_next = jnp.where(is_last_lane, beyond, lefts[i])
                        lefts[i] = beyond
                        right = pltpu.roll(u, 1, 1)
                        before = rights[i] if c else (u if k == 1 else 0.0)
                        x_prev = jnp.where(is_first_lane, before, right)
                        rights[i] = right
                        new = 0.5 * u - 0.125 * ((y_next + y_prev) + (x_next + x_prev))
                        fresh[side, j, k, r, s] = new
                        outgoing[side, k, r, s] += weight * new
                    column = after
            return carry

        return lax.fori_loop(0, TERMS, term, carry)

    lax.fori_loop(0, 2, part, 0)
    middle.wait()
    for copy in outer:
        copy.wait()


def close_kernel(dims, zero_halo, low, high, outgoing):
    nz, ny, nx = dims
    for side in range(2):
        for k in range(2):
            outgoing[side, k] = zero_halo[side, k]
            for source, r in ((low, slice(0, 1)), (high, slice(ny - 1, ny))):
                total = 0.0
                for j in range(TERMS):
                    total = total + (0.125 * pade_weights[j]) * source[side * TERMS + j, k : k + 1, :]
                outgoing[side, k, r, :] = zero_halo[side, k, r, :] - total


def store_kernel(dims, fresh, low, high, out, edges, sem):
    nz, ny, nx = dims
    inner = pl.ds(SUB, ny - 2 * SUB)
    middle = pltpu.make_async_copy(fresh.at[:, :, :, inner], out.at[0, :, :, :, inner], sem.at[0])
    middle.start()
    _, _, is_first_sub, is_last_sub = lane_masks()
    for side in range(2):
        for j in range(TERMS):
            for k in range(2):
                at = side * TERMS + j
                for c in range(nx // LANE):
                    s = slice(c * LANE, (c + 1) * LANE)
                    first = jnp.where(is_first_sub, 0.125 * low[at, k : k + 1, s], 0.0)
                    last = jnp.where(is_last_sub, 0.125 * high[at, k : k + 1, s], 0.0)
                    edges[0, side, j, k, :, s] = fresh[side, j, k, 0:SUB, s] - first
                    edges[1, side, j, k, :, s] = fresh[side, j, k, ny - SUB : ny, s] - last
    outer = [
        pltpu.make_async_copy(edges.at[e], out.at[0, :, :, :, pl.ds(start, SUB)], sem.at[1 + e])
        for e, start in enumerate((0, ny - SUB))
    ]
    for copy in outer:
        copy.start()
    middle.wait()
    for copy in outer:
        copy.wait()


def shift_up(block, axis):
    count = lax.axis_size(axis)
    return lax.ppermute(block, axis, [(i, i + 1) for i in range(count - 1)])


def shift_down(block, axis):
    count = lax.axis_size(axis)
    return lax.ppermute(block, axis, [(i + 1, i) for i in range(count - 1)])


def shards(electric, current, mass, faces, aux):
    nz, ny, nx = mass.shape
    dims = (nz, ny, nx)
    cells = nz * ny * nx
    bind = functools.partial
    rows_shape = (shape(nz, 2, nx),) * 2
    dma = pltpu.SemaphoreType.DMA
    electric, current, mass, faces, aux = (
        pltpu.with_memory_space_constraint(a, pltpu.HBM) for a in (electric, current, mass, faces, aux)
    )

    up1, down1 = pl.pallas_call(
        bind(pack_kernel, dims),
        out_shape=rows_shape,
        in_specs=[HBM] * 2,
        out_specs=(VM,) * 2,
        scratch_shapes=[vm(3, nz, SUB, nx), vm(3, nz, SUB, nx), vm(SUB, nx), dma((3,))],
        compiler_params=params(12),
        name="pack",
    )(electric, faces)
    low1 = shift_up(up1, "tile")
    high1 = shift_down(down1, "tile")

    field, current_v, weight, ghost, aux_v = pl.pallas_call(
        bind(first_kernel, dims),
        out_shape=(
            shape(3, nz + 1, ny, nx),
            shape(3, nz, ny, nx),
            shape(nz, ny, nx),
            shape(2, ny, nx),
            shape(2, TERMS, 2, ny, nx),
        ),
        in_specs=[HBM] * 5,
        out_specs=(VM,) * 5,
        scratch_shapes=[vm(ny, nx), vm(ny, nx), dma((nz,)), dma((nz,)), dma((nz,)), dma((4,))],
        compiler_params=params(24),
        cost_estimate=cost(45 * cells, 28 * cells),
        name="first_sweep",
    )(electric, current, mass, faces, aux)

    heads, tails = shape(nz + 1, 2, nx), shape(nz + 1, 3, nx)
    head, tail, up2, down2 = pl.pallas_call(
        bind(fix_pack_kernel, dims),
        out_shape=(heads, tails) + rows_shape,
        in_specs=[VM] * 4,
        out_specs=(VM,) * 4,
        compiler_params=params(16),
        name="fix_pack",
    )(field, weight, low1, high1)
    low2 = shift_up(up2, "tile")
    high2 = shift_down(down2, "tile")

    field = pl.pallas_call(
        bind(second_kernel, dims),
        out_shape=shape(3, nz, ny, nx),
        in_specs=[VM] * 6,
        out_specs=VM,
        scratch_shapes=[vm(ny, nx), vm(ny, nx)],
        compiler_params=params(24),
        cost_estimate=cost(40 * cells, 28 * cells),
        name="second_sweep",
    )(field, current_v, weight, ghost, head, tail)

    head, tail, traces, up3, down3 = pl.pallas_call(
        bind(fix_trace_kernel, dims),
        out_shape=(heads, tails, shape(2, 2, ny, nx)) + (shape(2 * TERMS, 2, nx),) * 2,
        in_specs=[VM] * 5,
        out_specs=(VM,) * 5,
        compiler_params=params(16),
        name="fix_trace",
    )(field, weight, aux_v, low2, high2)
    low3 = shift_up(up3, "tile")
    high3 = shift_down(down3, "tile")

    smoothed, fresh, outgoing = pl.pallas_call(
        bind(surface_kernel, dims),
        out_shape=(shape(3, nz, ny, nx), shape(2, TERMS, 2, ny, nx), shape(2, 2, ny, nx)),
        in_specs=[VM] * 5,
        out_specs=(HBM, VM, VM),
        scratch_shapes=[vm(2, 3, nz, SUB, nx), dma((3,))],
        compiler_params=params(24),
        cost_estimate=cost(20 * 16 * ny * nx, 12 * cells),
        name="surface",
    )(field, head, tail, traces, aux_v)

    outgoing = pl.pallas_call(
        bind(close_kernel, dims),
        out_shape=shape(2, 2, ny, nx),
        in_specs=[VM] * 3,
        out_specs=VM,
        compiler_params=params(8),
        name="close",
    )(outgoing, low3, high3)
    from_below = shift_up(outgoing[1], "slab")
    from_above = shift_down(outgoing[0], "slab")

    fresh = pl.pallas_call(
        bind(store_kernel, dims),
        out_shape=shape(1, 2, TERMS, 2, ny, nx),
        in_specs=[VM] * 3,
        out_specs=HBM,
        scratch_shapes=[vm(2, 2, TERMS, 2, SUB, nx), dma((3,))],
        compiler_params=params(8),
        cost_estimate=cost(16 * ny * nx, 8 * 16 * ny * nx),
        name="store",
    )(fresh, low3, high3)
    return smoothed, jnp.stack([from_below, from_above])[None], fresh


def solution(mesh):
    placed = (
        P(None, "slab", "tile", None),
        P(None, "slab", "tile", None),
        P("slab", "tile", None),
        P("slab", None, None, "tile", None),
        P("slab", None, None, None, "tile", None),
    )
    return jax.shard_map(
        shards,
        mesh=mesh,
        in_specs=placed,
        out_specs=(
            P(None, "slab", "tile", None),
            P("slab", None, None, "tile", None),
            P("slab", None, None, None, "tile", None),
        ),
        check_vma=False,
    )
```

```python
import functools
import math

import jax
import jax.numpy as jnp
from jax import lax
from jax.experimental import pallas as pl
from jax.experimental.pallas import tpu as pltpu
from jax.sharding import PartitionSpec as P


pade_weights = [2.0 / 9.0 * math.sin(j * math.pi / 9.0) ** 2 for j in range(1, 5)]
pade_decays = [math.cos(j * math.pi / 9.0) ** 2 for j in range(1, 5)]
TERMS = 4
SUB, LANE = 8, 128
F32 = jnp.float32
HBM = pl.BlockSpec(memory_space=pltpu.HBM)
VM = pl.BlockSpec(memory_space=pltpu.VMEM)


def params(mib):
    return pltpu.CompilerParams(vmem_limit_bytes=mib << 20)


def shape(*dims):
    return jax.ShapeDtypeStruct(dims, F32)


def cost(flops, count):
    return pl.CostEstimate(flops=flops, bytes_accessed=count, transcendentals=0)


def vm(*dims):
    return pltpu.VMEM(dims, F32)


def row_next(row):
    n = row.shape[1]
    at = lax.broadcasted_iota(jnp.int32, row.shape, 1)
    return jnp.where(at == n - 1, 0.0, pltpu.roll(row, n - 1, 1))


def row_prev(row):
    at = lax.broadcasted_iota(jnp.int32, row.shape, 1)
    return jnp.where(at == 0, 0.0, pltpu.roll(row, 1, 1))


def is_even(axis):
    return lax.rem(lax.axis_index(axis), 2) == 0


class Either:
    def __init__(self, choose, first, second):
        self.choose, self.first, self.second = choose, first, second

    def __getitem__(self, at):
        return jnp.where(self.choose, self.first[at], self.second[at])


def halo_views(near, far):
    even = is_even("tile")
    return Either(even, far, near), Either(even, near, far)


def upward(last, y_above):
    x, y, z = last
    return row_next(y) - y + x, z + (y_above - y)


def fixed_first(field, weight, low, z, zz):
    w = weight[z, 0:1, :]
    return field[0, zz, 0:1, :] + w * low[z, 0:1, :], field[2, zz, 0:1, :] + w * low[z, 1:2, :]


def fixed_last(field, weight, high, z, zz, ny):
    end = slice(ny - 1, ny)
    w = weight[z, end, :]
    hx, hz = high[z, 0:1, :], high[z, 1:2, :]
    rise = hz - high[z - 1, 1:2, :] if z else hz
    return (
        field[0, zz, end, :] + w * hx,
        field[1, zz, end, :] - w * (rise + (hx - row_prev(hx))),
        field[2, zz, end, :] + w * hz,
    )


def lane_masks():
    lane = lax.broadcasted_iota(jnp.int32, (SUB, LANE), 1)
    sub = lax.broadcasted_iota(jnp.int32, (SUB, LANE), 0)
    return lane == 0, lane == LANE - 1, sub == 0, sub == SUB - 1


def tile_at(i, c):
    return slice(i * SUB, (i + 1) * SUB), slice(c * LANE, (c + 1) * LANE)


def pack_kernel(dims, electric, faces, far, block, top, sem):
    nz, ny, _ = dims
    even = is_even("tile")
    start = pl.multiple_of(jnp.where(even, 0, ny - SUB), SUB)
    copies = [
        pltpu.make_async_copy(electric.at[:, :, pl.ds(start, SUB)], block, sem.at[0]),
        pltpu.make_async_copy(faces.at[0, 1, 1, pl.ds(ny - SUB, SUB)], top, sem.at[1]),
    ]
    for copy in copies:
        copy.start()
    for copy in copies:
        copy.wait()
    end = slice(SUB - 1, SUB)
    for z in range(nz):
        y_above = block[1, z + 1, end, :] if z + 1 < nz else top[end, :]
        up = upward([block[k, z, end, :] for k in range(3)], y_above)
        for q in range(2):
            far[z, q : q + 1, :] = jnp.where(even, block[2 * q, z, 0:1, :], up[q])


def sweep_plane(load, above, current, weight, store, hx_s, hy_s, dims, from_mass):
    _, ny, nx = dims
    rows, cols = ny // SUB, nx // LANE
    is_first_lane, is_last_lane, is_first_sub, is_last_sub = lane_masks()

    def left(k, i, c):
        return pltpu.roll(load(k, i, c), LANE - 1, 1)

    lefts = {(k, i): left(k, i, 0) for k in (1, 2) for i in range(rows)}
    right_y, right_z = {}, {}
    for c in range(cols):
        here = [[load(k, i, c) for k in range(3)] for i in range(rows)]
        ups = [{k: pltpu.roll(here[i][k], SUB - 1, 0) for k in (0, 2)} for i in range(rows)]
        down_x = down_z = None
        for i in range(rows):
            r, s = tile_at(i, c)

            def y_next(k):
                return jnp.where(is_last_sub, ups[i + 1][k] if i + 1 < rows else 0.0, ups[i][k])

            def x_next(k):
                after = left(k, i, c + 1) if c + 1 < cols else 0.0
                value = jnp.where(is_last_lane, after, lefts[k, i])
                lefts[k, i] = after
                return value

            ex, ey, ez = here[i]
            hx = (y_next(2) - ez) - (above(1, i, c) - ey)
            hy = (above(0, i, c) - ex) - (x_next(2) - ez)
            hz = (x_next(1) - ey) - (y_next(0) - ex)
            hx_low, hy_low = hx_s[r, s], hy_s[r, s]
            hx_s[r, s] = hx
            hy_s[r, s] = hy
            dx = pltpu.roll(hx, 1, 0)
            dz = pltpu.roll(hz, 1, 0)
            hx_y = jnp.where(is_first_sub, ez if i == 0 else down_x, dx)
            hz_y = jnp.where(is_first_sub, -ex if i == 0 else down_z, dz)
            down_x, down_z = dx, dz
            ry = pltpu.roll(hy, 1, 1)
            rz = pltpu.roll(hz, 1, 1)
            hy_x = jnp.where(is_first_lane, 0.0 if c == 0 else right_y[i], ry)
            hz_x = jnp.where(is_first_lane, 0.0 if c == 0 else right_z[i], rz)
            right_y[i], right_z[i] = ry, rz
            cx = (hz - hz_y) - (hy - hy_low)
            cy = (hx - hx_low) - (hz - hz_x)
            cz = (hy - hy_x) - (hx - hx_y)
            w = weight[r, s]
            if from_mass:
                w = 0.5 / (w + 4.0)
                weight[r, s] = w
            keep = 4.0 * w + 0.5
            store(0, i, c, keep * ex + w * (current(0, i, c) - cx))
            store(1, i, c, keep * ey + w * (current(1, i, c) - cy))
            store(2, i, c, keep * ez + w * (current(2, i, c) - cz))


def reader(ref, z):
    def load(k, i, c):
        r, s = tile_at(i, c)
        return ref[k, z, r, s]

    return load


def writer(ref, z):
    def store(k, i, c, value):
        r, s = tile_at(i, c)
        ref[k, z, r, s] = value

    return store


def ghost_flux(load, ghost, hx_s, hy_s, dims):
    _, ny, nx = dims
    for i in range(ny // SUB):
        for c in range(nx // LANE):
            r, s = tile_at(i, c)
            hx_s[r, s] = ghost[1, r, s] - load(1, i, c)
            hy_s[r, s] = load(0, i, c) - ghost[0, r, s]


def first_lower_kernel(
    dims, electric, current_h, mass, faces, aux_h,
    field, current, weight, ghost, aux, flux, near,
    field_sem, current_sem, weight_sem, face_sem,
):
    nz, ny, _ = dims
    half = nz // 2
    even = is_even("tile")
    end = slice(ny - 1, ny)
    copy = pltpu.make_async_copy

    def field_copy(z):
        return copy(electric.at[:, pl.ds(z, 1)], field.at[:, pl.ds(z, 1)], field_sem.at[z])

    def current_copy(z):
        return copy(current_h.at[:, pl.ds(z, 1)], current.at[:, pl.ds(z, 1)], current_sem.at[z])

    def weight_copy(z):
        return copy(mass.at[pl.ds(z, 1)], weight.at[pl.ds(z, 1)], weight_sem.at[z])

    low_copy = copy(faces.at[0, 0], ghost, face_sem.at[0])
    high_copies = [copy(faces.at[0, 1, k], field.at[k, nz], face_sem.at[1 + k]) for k in range(2)]
    aux_copy = copy(aux_h.at[0], aux, face_sem.at[3])
    low_copy.start()
    field_copy(0).start()

    def start(z, carry):
        field_copy(z + 1).start()
        current_copy(z).start()
        weight_copy(z).start()
        return carry

    lax.fori_loop(0, nz - 1, start, 0)
    current_copy(nz - 1).start()
    weight_copy(nz - 1).start()
    for high in high_copies:
        high.start()
    aux_copy.start()

    def pack(z):
        up = upward([field[k, z, end, :] for k in range(3)], field[1, z + 1, end, :])
        for q in range(2):
            near[z, q : q + 1, :] = jnp.where(even, up[q], field[2 * q, z, 0:1, :])

    low_copy.wait()
    field_copy(0).wait()
    hx_s, hy_s = flux.at[0], flux.at[1]
    ghost_flux(reader(field, 0), ghost, hx_s, hy_s, dims)

    def plane(z, carry):
        field_copy(z + 1).wait()
        pack(z)
        current_copy(z).wait()
        weight_copy(z).wait()
        sweep_plane(
            reader(field, z), reader(field, z + 1), reader(current, z), weight.at[z], writer(field, z), hx_s, hy_s, dims, True
        )
        return carry

    lax.fori_loop(0, half, plane, 0)

    def rest(z, carry):
        field_copy(z + 1).wait()
        pack(z)
        current_copy(z).wait()
        weight_copy(z).wait()
        return carry

    lax.fori_loop(half, nz - 1, rest, 0)
    for high in high_copies:
        high.wait()
    pack(nz - 1)
    current_copy(nz - 1).wait()
    weight_copy(nz - 1).wait()
    aux_copy.wait()


def first_upper_kernel(dims, old, current, mass, flux, field, weight, flux_s):
    nz, _, _ = dims
    half = nz // 2
    flux_s[...] = flux[...]
    for k in range(2):
        field[k, nz - half] = old[k, nz]

    def plane(z, carry):
        weight[z] = mass[z + half]
        sweep_plane(
            reader(old, z + half), reader(old, z + half + 1), reader(current, z + half),
            weight.at[z], writer(field, z), flux_s.at[0], flux_s.at[1], dims, True,
        )
        return carry

    lax.fori_loop(0, nz - half, plane, 0)


class Planes:
    def __init__(self, lower, upper, half, dim):
        self.lower, self.upper, self.half, self.dim = lower, upper, half, dim

    def __getitem__(self, at):
        z = at[self.dim]
        if z < self.half:
            return self.lower[at]
        return self.upper[at[: self.dim] + (z - self.half,) + at[self.dim + 1 :]]


def fix_pack_kernel(dims, field_a, field_b, weight_a, weight_b, near, far, head, tail, far_next):
    nz, ny, _ = dims
    half = nz // 2
    even = is_even("tile")
    end = slice(ny - 1, ny)
    field = Planes(field_a, field_b, half, 1)
    weight = Planes(weight_a, weight_b, half, 0)
    low, high = halo_views(near, far)
    for z in range(nz):
        head[z, 0:1, :], head[z, 1:2, :] = fixed_first(field, weight, low, z, z)
        x, y, zc = fixed_last(field, weight, high, z, z, ny)
        tail[z, 0:1, :], tail[z, 1:2, :], tail[z, 2:3, :] = x, y, zc
    head[nz, 0:1, :] = field[0, nz, 0:1, :]
    tail[nz, 0:1, :] = field[0, nz, end, :]
    tail[nz, 1:2, :] = field[1, nz, end, :]
    for z in range(nz):
        up = upward([tail[z, k : k + 1, :] for k in range(3)], tail[z + 1, 1:2, :])
        for q in range(2):
            far_next[z, q : q + 1, :] = jnp.where(even, head[z, q : q + 1, :], up[q])


def edged_reader(ref, z, head, tail, plane, ny):
    rows = ny // SUB
    _, _, is_first_sub, is_last_sub = lane_masks()

    def load(k, i, c):
        r, s = tile_at(i, c)
        value = ref[k, z, r, s]
        if i == 0 and k != 1:
            value = jnp.where(is_first_sub, head[plane, k // 2 : k // 2 + 1, s], value)
        if i == rows - 1:
            value = jnp.where(is_last_sub, tail[plane, k : k + 1, s], value)
        return value

    return load


def second_lower_kernel(dims, old_a, old_b, current, weight, ghost, head, tail, field, flux, near_next):
    nz, ny, _ = dims
    half = nz // 2
    even = is_even("tile")
    for z in range(nz):
        up = upward([tail[z, k : k + 1, :] for k in range(3)], tail[z + 1, 1:2, :])
        for q in range(2):
            near_next[z, q : q + 1, :] = jnp.where(even, up[q], head[z, q : q + 1, :])
    hx_s, hy_s = flux.at[0], flux.at[1]
    ghost_flux(edged_reader(old_a, 0, head, tail, 0, ny), ghost, hx_s, hy_s, dims)

    def sweep(z, above):
        sweep_plane(
            edged_reader(old_a, z, head, tail, z, ny), above, reader(current, z), weight.at[z],
            writer(field, z), hx_s, hy_s, dims, False,
        )

    def plane(z, carry):
        sweep(z, edged_reader(old_a, z + 1, head, tail, z + 1, ny))
        return carry

    lax.fori_loop(0, half - 1, plane, 0)
    sweep(half - 1, edged_reader(old_b, 0, head, tail, half, ny))


def second_upper_kernel(dims, old, current, weight, flux, head, tail, field, flux_s):
    nz, ny, _ = dims
    half = nz // 2
    flux_s[...] = flux[...]

    def plane(z, carry):
        at = z + half
        sweep_plane(
            edged_reader(old, z, head, tail, at, ny), edged_reader(old, z + 1, head, tail, at + 1, ny),
            reader(current, at), weight.at[z], writer(field, z), flux_s.at[0], flux_s.at[1], dims, False,
        )
        return carry

    lax.fori_loop(0, nz - half, plane, 0)


def fix_trace_kernel(
    dims, field_a, field_b, weight_a, weight_b, aux, near, far, head, tail, traces, far_next
):
    nz, ny, _ = dims
    half = nz // 2
    even = is_even("tile")
    end = slice(ny - 1, ny)
    field = Planes(field_a, field_b, half, 1)
    weight = Planes(weight_a, weight_b, half, 0)
    low, high = halo_views(near, far)
    for side in range(2):
        z = (nz - 1) * side
        for k in range(2):
            traces[side, k] = field[k, z]
    for z in range(nz):
        head[z, 0:1, :], head[z, 1:2, :] = fixed_first(field, weight, low, z, z)
        x, y, zc = fixed_last(field, weight, high, z, z, ny)
        tail[z, 0:1, :], tail[z, 1:2, :], tail[z, 2:3, :] = x, y, zc
        if z in (0, nz - 1):
            side = 0 if z == 0 else 1
            traces[side, 0, 0:1, :] = head[z, 0:1, :]
            traces[side, 0, end, :] = x
            traces[side, 1, end, :] = y
    pack_combined(even, traces, aux, far_next, ny, False)


def pack_combined(even, traces, aux, send, ny, up_from_even):
    end = slice(ny - 1, ny)
    for side in range(2):
        for k in range(2):
            first = traces[side, k, 0:1, :]
            last = traces[side, k, end, :]
            for j in range(TERMS):
                down = first - pade_decays[j] * aux[side, j, k, 0:1, :]
                up = last - pade_decays[j] * aux[side, j, k, end, :]
                pair = (up, down) if up_from_even else (down, up)
                send[side * TERMS + j, k : k + 1, :] = jnp.where(even, *pair)


def surface_kernel(dims, traces, aux, fresh, outgoing, near_next):
    _, ny, nx = dims
    rows, cols = ny // SUB, nx // LANE
    is_first_lane, is_last_lane, is_first_sub, is_last_sub = lane_masks()
    pack_combined(is_even("tile"), traces, aux, near_next, ny, True)

    def part(side, carry):
        outgoing[side] = traces[side]

        def term(j, carry):
            decay = weight = F32(0.0)
            for q in range(TERMS):
                decay = jnp.where(j == q, F32(pade_decays[q]), decay)
                weight = jnp.where(j == q, F32(pade_weights[q]), weight)
            for k in range(2):

                def value(i, c):
                    r, s = tile_at(i, c)
                    return traces[side, k, r, s] - decay * aux[side, j, k, r, s]

                column = [value(i, 0) for i in range(rows)]
                lefts = [pltpu.roll(u, LANE - 1, 1) for u in column]
                rights = [0.0] * rows
                for c in range(cols):
                    ups = [pltpu.roll(u, SUB - 1, 0) for u in column]
                    downs = [pltpu.roll(u, 1, 0) for u in column]
                    after = [value(i, c + 1) for i in range(rows)] if c + 1 < cols else None
                    for i in range(rows):
                        r, s = tile_at(i, c)
                        u = column[i]
                        y_next = jnp.where(is_last_sub, ups[i + 1] if i + 1 < rows else 0.0, ups[i])
                        y_prev = jnp.where(is_first_sub, downs[i - 1] if i else 0.0, downs[i])
                        if after is not None:
                            beyond = pltpu.roll(after[i], LANE - 1, 1)
                        else:
                            beyond = u if k == 0 else 0.0
                        x_next = jnp.where(is_last_lane, beyond, lefts[i])
                        lefts[i] = beyond
                        right = pltpu.roll(u, 1, 1)
                        before = rights[i] if c else (u if k == 1 else 0.0)
                        x_prev = jnp.where(is_first_lane, before, right)
                        rights[i] = right
                        new = 0.5 * u - 0.125 * ((y_next + y_prev) + (x_next + x_prev))
                        fresh[side, j, k, r, s] = new
                        outgoing[side, k, r, s] += weight * new
                    column = after
            return carry

        return lax.fori_loop(0, TERMS, term, carry)

    lax.fori_loop(0, 2, part, 0)


def write_kernel(dims, field_a, field_b, head, tail, smoothed, edges, sem):
    nz, ny, nx = dims
    half = nz // 2
    _, _, is_first_sub, is_last_sub = lane_masks()
    inner = pl.ds(SUB, ny - 2 * SUB)
    copies = []
    for n, (field, start, count) in enumerate(((field_a, 0, half), (field_b, half, nz - half))):
        planes = pl.ds(start, count)
        copies.append(pltpu.make_async_copy(field.at[:, :, inner], smoothed.at[:, planes, inner], sem.at[n]))
        copies[-1].start()
    for n, (field, start, count) in enumerate(((field_a, 0, half), (field_b, half, nz - half))):

        def merge(z, carry):
            at = z + start
            for c in range(nx // LANE):
                s = slice(c * LANE, (c + 1) * LANE)
                for k in range(3):
                    value = field[k, z, 0:SUB, s]
                    if k != 1:
                        value = jnp.where(is_first_sub, head[at, k // 2 : k // 2 + 1, s], value)
                    edges[0, k, at, :, s] = value
                    value = field[k, z, ny - SUB : ny, s]
                    edges[1, k, at, :, s] = jnp.where(is_last_sub, tail[at, k : k + 1, s], value)
            return carry

        lax.fori_loop(0, count, merge, 0)
        planes = pl.ds(start, count)
        for e, row in enumerate((0, ny - SUB)):
            copies.append(
                pltpu.make_async_copy(
                    edges.at[e, :, planes], smoothed.at[:, planes, pl.ds(row, SUB)], sem.at[2 + 2 * n + e]
                )
            )
            copies[-1].start()
    for copy in copies:
        copy.wait()


def close_kernel(dims, zero_halo, near, far, even_side, odd_side, outgoing):
    _, ny, _ = dims
    low, high = halo_views(near, far)
    for side in range(2):
        for k in range(2):
            outgoing[side, k] = zero_halo[side, k]
            for source, r in ((low, slice(0, 1)), (high, slice(ny - 1, ny))):
                total = 0.0
                for j in range(TERMS):
                    total = total + (0.125 * pade_weights[j]) * source[side * TERMS + j, k : k + 1, :]
                outgoing[side, k, r, :] = zero_halo[side, k, r, :] - total
    even = is_even("slab")
    even_side[...] = jnp.where(even, outgoing[1], outgoing[0])
    odd_side[...] = jnp.where(even, outgoing[0], outgoing[1])


def faces_kernel(even_side, odd_side, out, sem):
    below = jnp.where(is_even("slab"), 0, 1)
    copies = [
        pltpu.make_async_copy(odd_side, out.at[0, below], sem.at[0]),
        pltpu.make_async_copy(even_side, out.at[0, 1 - below], sem.at[1]),
    ]
    for copy in copies:
        copy.start()
    for copy in copies:
        copy.wait()


def store_kernel(dims, fresh, near, far, out, edges, sem):
    _, ny, nx = dims
    low, high = halo_views(near, far)
    inner = pl.ds(SUB, ny - 2 * SUB)
    middle = pltpu.make_async_copy(fresh.at[:, :, :, inner], out.at[0, :, :, :, inner], sem.at[0])
    middle.start()
    _, _, is_first_sub, is_last_sub = lane_masks()
    for side in range(2):
        for j in range(TERMS):
            for k in range(2):
                at = side * TERMS + j
                for c in range(nx // LANE):
                    s = slice(c * LANE, (c + 1) * LANE)
                    first = jnp.where(is_first_sub, 0.125 * low[at, k : k + 1, s], 0.0)
                    last = jnp.where(is_last_sub, 0.125 * high[at, k : k + 1, s], 0.0)
                    edges[0, side, j, k, :, s] = fresh[side, j, k, 0:SUB, s] - first
                    edges[1, side, j, k, :, s] = fresh[side, j, k, ny - SUB : ny, s] - last
    outer = [
        pltpu.make_async_copy(edges.at[e], out.at[0, :, :, :, pl.ds(start, SUB)], sem.at[1 + e])
        for e, start in enumerate((0, ny - SUB))
    ]
    for copy in outer:
        copy.start()
    middle.wait()
    for copy in outer:
        copy.wait()


def call(kernel, **options):
    return pl.pallas_call(kernel, **options)


def swap(block, axis, first):
    pairs = [(i, i + 1) for i in range(first, lax.axis_size(axis) - 1, 2)]
    return lax.ppermute(block, axis, [p for i, j in pairs for p in ((i, j), (j, i))])


def iteration(electric, current, mass, faces, aux):
    nz, ny, nx = mass.shape
    half = nz // 2
    dims = (nz, ny, nx)
    cells = nz * ny * nx
    bind = functools.partial
    rows = shape(nz, 2, nx)
    flux_shape = shape(2, ny, nx)
    dma = pltpu.SemaphoreType.DMA
    electric, current, mass, faces, aux = (
        pltpu.with_memory_space_constraint(a, pltpu.HBM) for a in (electric, current, mass, faces, aux)
    )

    far1 = call(
        bind(pack_kernel, dims),
        out_shape=rows,
        in_specs=[HBM] * 2,
        out_specs=VM,
        scratch_shapes=[vm(3, nz, SUB, nx), vm(SUB, nx), dma((2,))],
        compiler_params=params(12),
    )(electric, faces)
    far1 = swap(far1, "tile", 1)

    field, current_v, weight, ghost, aux_v, flux, near1 = call(
        bind(first_lower_kernel, dims),
        out_shape=(
            shape(3, nz + 1, ny, nx),
            shape(3, nz, ny, nx),
            shape(nz, ny, nx),
            shape(2, ny, nx),
            shape(2, TERMS, 2, ny, nx),
            flux_shape,
            rows,
        ),
        in_specs=[HBM] * 5,
        out_specs=(VM,) * 7,
        scratch_shapes=[dma((nz,)), dma((nz,)), dma((nz,)), dma((4,))],
        compiler_params=params(24),
        cost_estimate=cost(25 * cells, 28 * cells),
    )(electric, current, mass, faces, aux)
    near1 = swap(near1, "tile", 0)

    upper, weight_u = call(
        bind(first_upper_kernel, dims),
        out_shape=(shape(3, nz - half + 1, ny, nx), shape(nz - half, ny, nx)),
        in_specs=[VM] * 4,
        out_specs=(VM,) * 2,
        scratch_shapes=[vm(2, ny, nx)],
        compiler_params=params(12),
        cost_estimate=cost(25 * cells, 14 * cells),
    )(field, current_v, weight, flux)

    heads, tails = shape(nz + 1, 2, nx), shape(nz + 1, 3, nx)
    head, tail, far2 = call(
        bind(fix_pack_kernel, dims),
        out_shape=(heads, tails, rows),
        in_specs=[VM] * 6,
        out_specs=(VM,) * 3,
        compiler_params=params(12),
    )(field, upper, weight, weight_u, near1, far1)
    far2 = swap(far2, "tile", 1)

    lower2, flux, near2 = call(
        bind(second_lower_kernel, dims),
        out_shape=(shape(3, half, ny, nx), flux_shape, rows),
        in_specs=[VM] * 7,
        out_specs=(VM,) * 3,
        compiler_params=params(12),
        cost_estimate=cost(20 * cells, 14 * cells),
    )(field, upper, current_v, weight, ghost, head, tail)
    near2 = swap(near2, "tile", 0)

    upper2 = call(
        bind(second_upper_kernel, dims),
        out_shape=shape(3, nz - half, ny, nx),
        in_specs=[VM] * 6,
        out_specs=VM,
        scratch_shapes=[vm(2, ny, nx)],
        compiler_params=params(12),
        cost_estimate=cost(20 * cells, 14 * cells),
    )(upper, current_v, weight_u, flux, head, tail)

    edge_rows = shape(2 * TERMS, 2, nx)
    head, tail, traces, far3 = call(
        bind(fix_trace_kernel, dims),
        out_shape=(heads, tails, shape(2, 2, ny, nx), edge_rows),
        in_specs=[VM] * 7,
        out_specs=(VM,) * 4,
        compiler_params=params(12),
    )(lower2, upper2, weight, weight_u, aux_v, near2, far2)
    far3 = swap(far3, "tile", 1)

    fresh, outgoing, near3 = call(
        bind(surface_kernel, dims),
        out_shape=(shape(2, TERMS, 2, ny, nx), shape(2, 2, ny, nx), edge_rows),
        in_specs=[VM] * 2,
        out_specs=(VM,) * 3,
        compiler_params=params(12),
        cost_estimate=cost(20 * 16 * ny * nx, 12 * cells),
    )(traces, aux_v)
    near3 = swap(near3, "tile", 0)

    smoothed = call(
        bind(write_kernel, dims),
        out_shape=shape(3, nz, ny, nx),
        in_specs=[VM] * 4,
        out_specs=HBM,
        scratch_shapes=[vm(2, 3, nz, SUB, nx), dma((6,))],
        compiler_params=params(12),
        cost_estimate=cost(cells, 12 * cells),
    )(lower2, upper2, head, tail)

    side_shape = shape(2, ny, nx)
    even_side, odd_side = call(
        bind(close_kernel, dims),
        out_shape=(side_shape, side_shape),
        in_specs=[VM] * 3,
        out_specs=(VM,) * 2,
        scratch_shapes=[vm(2, 2, ny, nx)],
        compiler_params=params(8),
    )(outgoing, near3, far3)
    odd_side = swap(odd_side, "slab", 1)
    even_side = swap(even_side, "slab", 0)

    fresh = call(
        bind(store_kernel, dims),
        out_shape=shape(1, 2, TERMS, 2, ny, nx),
        in_specs=[VM] * 3,
        out_specs=HBM,
        scratch_shapes=[vm(2, 2, TERMS, 2, SUB, nx), dma((3,))],
        compiler_params=params(8),
        cost_estimate=cost(16 * ny * nx, 8 * 16 * ny * nx),
    )(fresh, near3, far3)

    next_faces = call(
        faces_kernel,
        out_shape=shape(1, 2, 2, ny, nx),
        in_specs=[VM] * 2,
        out_specs=HBM,
        scratch_shapes=[dma((2,))],
        compiler_params=params(8),
    )(even_side, odd_side)
    return smoothed, next_faces, fresh


def solution(mesh):
    placed = (
        P(None, "slab", "tile", None),
        P(None, "slab", "tile", None),
        P("slab", "tile", None),
        P("slab", None, None, "tile", None),
        P("slab", None, None, None, "tile", None),
    )
    return jax.shard_map(
        iteration,
        mesh=mesh,
        in_specs=placed,
        out_specs=(
            P(None, "slab", "tile", None),
            P("slab", None, None, "tile", None),
            P("slab", None, None, None, "tile", None),
        ),
        check_vma=False,
    )
```

```python
import functools
import math

import jax
import jax.numpy as jnp
from jax import lax
from jax.experimental import pallas as pl
from jax.experimental.pallas import tpu as pltpu
from jax.sharding import PartitionSpec as P


pade_weights = [2.0 / 9.0 * math.sin(j * math.pi / 9.0) ** 2 for j in range(1, 5)]
pade_decays = [math.cos(j * math.pi / 9.0) ** 2 for j in range(1, 5)]
TERMS = 4
SUB, LANE = 8, 128
F32 = jnp.float32
HBM = pl.BlockSpec(memory_space=pltpu.HBM)
VM = pl.BlockSpec(memory_space=pltpu.VMEM)


def params(mib):
    return pltpu.CompilerParams(vmem_limit_bytes=mib << 20)


def shape(*dims):
    return jax.ShapeDtypeStruct(dims, F32)


def cost(flops, count):
    return pl.CostEstimate(flops=flops, bytes_accessed=count, transcendentals=0)


def vm(*dims):
    return pltpu.VMEM(dims, F32)


def row_next(row):
    n = row.shape[1]
    at = lax.broadcasted_iota(jnp.int32, row.shape, 1)
    return jnp.where(at == n - 1, 0.0, pltpu.roll(row, n - 1, 1))


def row_prev(row):
    at = lax.broadcasted_iota(jnp.int32, row.shape, 1)
    return jnp.where(at == 0, 0.0, pltpu.roll(row, 1, 1))


def is_even(axis):
    return lax.rem(lax.axis_index(axis), 2) == 0


class Either:
    def __init__(self, choose, first, second):
        self.choose, self.first, self.second = choose, first, second

    def __getitem__(self, at):
        return jnp.where(self.choose, self.first[at], self.second[at])


def halo_views(near, far):
    even = is_even("tile")
    return Either(even, far, near), Either(even, near, far)


def upward(last, y_above):
    x, y, z = last
    return row_next(y) - y + x, z + (y_above - y)


def fixed_first(field, weight, low, z, zz):
    w = weight[z, 0:1, :]
    return field[0, zz, 0:1, :] + w * low[z, 0:1, :], field[2, zz, 0:1, :] + w * low[z, 1:2, :]


def fixed_last(field, weight, high, z, zz, ny):
    end = slice(ny - 1, ny)
    w = weight[z, end, :]
    hx, hz = high[z, 0:1, :], high[z, 1:2, :]
    rise = hz - high[z - 1, 1:2, :] if z else hz
    return (
        field[0, zz, end, :] + w * hx,
        field[1, zz, end, :] - w * (rise + (hx - row_prev(hx))),
        field[2, zz, end, :] + w * hz,
    )


def lane_masks():
    lane = lax.broadcasted_iota(jnp.int32, (SUB, LANE), 1)
    sub = lax.broadcasted_iota(jnp.int32, (SUB, LANE), 0)
    return lane == 0, lane == LANE - 1, sub == 0, sub == SUB - 1


def tile_at(i, c):
    return slice(i * SUB, (i + 1) * SUB), slice(c * LANE, (c + 1) * LANE)


def pack_kernel(dims, electric, faces, aux, far, block, top, aux_block, sem):
    nz, ny, _ = dims
    even = is_even("tile")
    start = pl.multiple_of(jnp.where(even, 0, ny - SUB), SUB)
    copies = [
        pltpu.make_async_copy(electric.at[:, :, pl.ds(start, SUB)], block, sem.at[0]),
        pltpu.make_async_copy(faces.at[0, 1, 1, pl.ds(ny - SUB, SUB)], top, sem.at[1]),
        pltpu.make_async_copy(aux.at[0, :, :, :, pl.ds(start, SUB)], aux_block, sem.at[2]),
    ]
    for copy in copies:
        copy.start()
    for copy in copies:
        copy.wait()
    end = slice(SUB - 1, SUB)
    for z in range(nz):
        y_above = block[1, z + 1, end, :] if z + 1 < nz else top[end, :]
        up = upward([block[k, z, end, :] for k in range(3)], y_above)
        for q in range(2):
            far[z, q : q + 1, :] = jnp.where(even, block[2 * q, z, 0:1, :], up[q])
    for side in range(2):
        for j in range(TERMS):
            for k in range(2):
                far[nz + side * TERMS + j, k : k + 1, :] = jnp.where(
                    even, aux_block[side, j, k, 0:1, :], aux_block[side, j, k, end, :]
                )


def sweep_plane(load, above, current, weight, store, hx_s, hy_s, dims, from_mass):
    _, ny, nx = dims
    rows, cols = ny // SUB, nx // LANE
    is_first_lane, is_last_lane, is_first_sub, is_last_sub = lane_masks()

    def left(k, i, c):
        return pltpu.roll(load(k, i, c), LANE - 1, 1)

    lefts = {(k, i): left(k, i, 0) for k in (1, 2) for i in range(rows)}
    right_y, right_z = {}, {}
    for c in range(cols):
        here = [[load(k, i, c) for k in range(3)] for i in range(rows)]
        ups = [{k: pltpu.roll(here[i][k], SUB - 1, 0) for k in (0, 2)} for i in range(rows)]
        down_x = down_z = None
        for i in range(rows):
            r, s = tile_at(i, c)

            def y_next(k):
                return jnp.where(is_last_sub, ups[i + 1][k] if i + 1 < rows else 0.0, ups[i][k])

            def x_next(k):
                after = left(k, i, c + 1) if c + 1 < cols else 0.0
                value = jnp.where(is_last_lane, after, lefts[k, i])
                lefts[k, i] = after
                return value

            ex, ey, ez = here[i]
            hx = (y_next(2) - ez) - (above(1, i, c) - ey)
            hy = (above(0, i, c) - ex) - (x_next(2) - ez)
            hz = (x_next(1) - ey) - (y_next(0) - ex)
            hx_low, hy_low = hx_s[r, s], hy_s[r, s]
            hx_s[r, s] = hx
            hy_s[r, s] = hy
            dx = pltpu.roll(hx, 1, 0)
            dz = pltpu.roll(hz, 1, 0)
            hx_y = jnp.where(is_first_sub, ez if i == 0 else down_x, dx)
            hz_y = jnp.where(is_first_sub, -ex if i == 0 else down_z, dz)
            down_x, down_z = dx, dz
            ry = pltpu.roll(hy, 1, 1)
            rz = pltpu.roll(hz, 1, 1)
            hy_x = jnp.where(is_first_lane, 0.0 if c == 0 else right_y[i], ry)
            hz_x = jnp.where(is_first_lane, 0.0 if c == 0 else right_z[i], rz)
            right_y[i], right_z[i] = ry, rz
            cx = (hz - hz_y) - (hy - hy_low)
            cy = (hx - hx_low) - (hz - hz_x)
            cz = (hy - hy_x) - (hx - hx_y)
            w = weight[r, s]
            if from_mass:
                w = 0.5 / (w + 4.0)
                weight[r, s] = w
            keep = 4.0 * w + 0.5
            store(0, i, c, keep * ex + w * (current(0, i, c) - cx))
            store(1, i, c, keep * ey + w * (current(1, i, c) - cy))
            store(2, i, c, keep * ez + w * (current(2, i, c) - cz))


def reader(ref, z):
    def load(k, i, c):
        r, s = tile_at(i, c)
        return ref[k, z, r, s]

    return load


def writer(ref, z):
    def store(k, i, c, value):
        r, s = tile_at(i, c)
        ref[k, z, r, s] = value

    return store


def ghost_flux(load, ghost, hx_s, hy_s, dims):
    _, ny, nx = dims
    for i in range(ny // SUB):
        for c in range(nx // LANE):
            r, s = tile_at(i, c)
            hx_s[r, s] = ghost[1, r, s] - load(1, i, c)
            hy_s[r, s] = load(0, i, c) - ghost[0, r, s]


def first_lower_kernel(
    dims, electric, current_h, mass, faces, aux_h,
    field, current, weight, ghost, flux, near,
    block, top, aux_block, field_sem, current_sem, weight_sem, sem,
):
    nz, ny, _ = dims
    half = nz // 2
    even = is_even("tile")
    end = slice(ny - 1, ny)
    tile_end = slice(SUB - 1, SUB)
    copy = pltpu.make_async_copy
    row = pl.multiple_of(jnp.where(even, ny - SUB, 0), SUB)

    def field_copy(z):
        return copy(electric.at[:, pl.ds(z, 1)], field.at[:, pl.ds(z, 1)], field_sem.at[z])

    def current_copy(z):
        return copy(current_h.at[:, pl.ds(z, 1)], current.at[:, pl.ds(z, 1)], current_sem.at[z])

    def weight_copy(z):
        return copy(mass.at[pl.ds(z, 1)], weight.at[pl.ds(z, 1)], weight_sem.at[z])

    low_copy = copy(faces.at[0, 0], ghost, sem.at[0])
    edge_copies = [
        copy(electric.at[:, pl.ds(half, nz - half), pl.ds(row, SUB)], block, sem.at[1]),
        copy(faces.at[0, 1, 1, pl.ds(ny - SUB, SUB)], top, sem.at[2]),
        copy(aux_h.at[0, :, :, :, pl.ds(row, SUB)], aux_block, sem.at[3]),
    ]
    low_copy.start()
    field_copy(0).start()

    def start(z, carry):
        field_copy(z + 1).start()
        current_copy(z).start()
        weight_copy(z).start()
        return carry

    lax.fori_loop(0, half, start, 0)
    for edge in edge_copies:
        edge.start()

    low_copy.wait()
    field_copy(0).wait()
    hx_s, hy_s = flux.at[0], flux.at[1]
    ghost_flux(reader(field, 0), ghost, hx_s, hy_s, dims)

    def plane(z, carry):
        field_copy(z + 1).wait()
        up = upward([field[k, z, end, :] for k in range(3)], field[1, z + 1, end, :])
        for q in range(2):
            near[z, q : q + 1, :] = jnp.where(even, up[q], field[2 * q, z, 0:1, :])
        current_copy(z).wait()
        weight_copy(z).wait()
        sweep_plane(
            reader(field, z), reader(field, z + 1), reader(current, z), weight.at[z], writer(field, z), hx_s, hy_s, dims, True
        )
        return carry

    lax.fori_loop(0, half, plane, 0)
    for edge in edge_copies:
        edge.wait()
    for z in range(nz - half):
        y_above = block[1, z + 1, tile_end, :] if z + 1 < nz - half else top[tile_end, :]
        up = upward([block[k, z, tile_end, :] for k in range(3)], y_above)
        for q in range(2):
            near[half + z, q : q + 1, :] = jnp.where(even, up[q], block[2 * q, z, 0:1, :])
    for side in range(2):
        for j in range(TERMS):
            for k in range(2):
                near[nz + side * TERMS + j, k : k + 1, :] = jnp.where(
                    even, aux_block[side, j, k, tile_end, :], aux_block[side, j, k, 0:1, :]
                )


def first_upper_kernel(
    dims, electric, current_h, mass, faces, aux_h, flux,
    field, current, weight, aux,
    flux_s, field_sem, current_sem, weight_sem, sem,
):
    nz, _, _ = dims
    half = nz // 2
    count = nz - half
    copy = pltpu.make_async_copy

    def field_copy(z):
        return copy(electric.at[:, pl.ds(z + half, 1)], field.at[:, pl.ds(z, 1)], field_sem.at[z])

    def current_copy(z):
        return copy(current_h.at[:, pl.ds(z + half, 1)], current.at[:, pl.ds(z, 1)], current_sem.at[z])

    def weight_copy(z):
        return copy(mass.at[pl.ds(z + half, 1)], weight.at[pl.ds(z, 1)], weight_sem.at[z])

    high_copies = [copy(faces.at[0, 1, k], field.at[k, count], sem.at[k]) for k in range(2)]
    aux_copy = copy(aux_h.at[0], aux, sem.at[2])
    field_copy(0).start()

    def start(z, carry):
        field_copy(z + 1).start()
        current_copy(z).start()
        weight_copy(z).start()
        return carry

    lax.fori_loop(0, count - 1, start, 0)
    current_copy(count - 1).start()
    weight_copy(count - 1).start()
    for high in high_copies:
        high.start()
    aux_copy.start()
    flux_s[...] = flux[...]
    field_copy(0).wait()

    def plane(z, carry):
        @pl.when(z + 1 < count)
        def _():
            field_copy(z + 1).wait()

        @pl.when(z + 1 == count)
        def _():
            for high in high_copies:
                high.wait()

        current_copy(z).wait()
        weight_copy(z).wait()
        sweep_plane(
            reader(field, z), reader(field, z + 1), reader(current, z),
            weight.at[z], writer(field, z), flux_s.at[0], flux_s.at[1], dims, True,
        )
        return carry

    lax.fori_loop(0, count, plane, 0)
    aux_copy.wait()


class Planes:
    def __init__(self, lower, upper, half, dim):
        self.lower, self.upper, self.half, self.dim = lower, upper, half, dim

    def __getitem__(self, at):
        z = at[self.dim]
        if z < self.half:
            return self.lower[at]
        return self.upper[at[: self.dim] + (z - self.half,) + at[self.dim + 1 :]]


def fix_pack_kernel(
    dims, field_a, field_b, current_a, current_b, weight_a, weight_b, ghost, near, far,
    head, tail, far_next, near_extra,
):
    nz, ny, nx = dims
    half = nz // 2
    even = is_even("tile")
    end = slice(ny - 1, ny)
    field = Planes(field_a, field_b, half, 1)
    current = Planes(current_a, current_b, half, 1)
    weight = Planes(weight_a, weight_b, half, 0)
    low, high = halo_views(near, far)
    for z in range(nz):
        head[z, 0:1, :], head[z, 1:2, :] = fixed_first(field, weight, low, z, z)
        x, y, zc = fixed_last(field, weight, high, z, z, ny)
        tail[z, 0:1, :], tail[z, 1:2, :], tail[z, 2:3, :] = x, y, zc
    head[nz, 0:1, :] = field[0, nz, 0:1, :]
    tail[nz, 0:1, :] = field[0, nz, end, :]
    tail[nz, 1:2, :] = field[1, nz, end, :]
    for z in range(nz):
        up = upward([tail[z, k : k + 1, :] for k in range(3)], tail[z + 1, 1:2, :])
        for q in range(2):
            far_next[z, q : q + 1, :] = jnp.where(even, head[z, q : q + 1, :], up[q])

    def value(k, z, r):
        at = slice(r, r + 1)
        if r in (-1, ny) or (k == 2 and z in (-1, nz)):
            return jnp.zeros((1, nx), F32)
        if z == -1:
            return ghost[k, at, :]
        if r == 0 and k != 1:
            return head[z, k // 2 : k // 2 + 1, :]
        if r == ny - 1:
            return tail[z, k : k + 1, :]
        return field[k, z, at, :]

    def flux_x(z, r):
        return (value(2, z, r + 1) - value(2, z, r)) - (value(1, z + 1, r) - value(1, z, r))

    def flux_y(z, r):
        here = value(2, z, r)
        return (value(0, z + 1, r) - value(0, z, r)) - (row_next(here) - here)

    def flux_z(z, r):
        here = value(1, z, r)
        return (row_next(here) - here) - (value(0, z, r + 1) - value(0, z, r))

    def trace(z, r):
        at = slice(r, r + 1)
        hz = flux_z(z, r)
        cx = (hz - flux_z(z, r - 1)) - (flux_y(z, r) - flux_y(z - 1, r))
        cy = (flux_x(z, r) - flux_x(z - 1, r)) - (hz - row_prev(hz))
        w = weight[z, at, :]
        keep = 4.0 * w + 0.5
        return (
            keep * value(0, z, r) + w * (current[0, z, at, :] - cx),
            keep * value(1, z, r) + w * (current[1, z, at, :] - cy),
            w,
        )

    for side in range(2):
        z = (nz - 1) * side
        down, up = trace(z, 0), trace(z, ny - 1)
        for k in range(2):
            far_next[nz + side, k : k + 1, :] = jnp.where(even, down[k], up[k])
            near_extra[side, k : k + 1, :] = jnp.where(even, up[k], down[k])
        far_next[nz + 2, side : side + 1, :] = jnp.where(even, down[2], up[2])
        near_extra[2, side : side + 1, :] = jnp.where(even, up[2], down[2])


def edged_reader(ref, z, head, tail, plane, ny):
    rows = ny // SUB
    _, _, is_first_sub, is_last_sub = lane_masks()

    def load(k, i, c):
        r, s = tile_at(i, c)
        value = ref[k, z, r, s]
        if i == 0 and k != 1:
            value = jnp.where(is_first_sub, head[plane, k // 2 : k // 2 + 1, s], value)
        if i == rows - 1:
            value = jnp.where(is_last_sub, tail[plane, k : k + 1, s], value)
        return value

    return load


def second_lower_kernel(
    dims, old_a, old_b, current, weight, ghost, head, tail, near_extra, field, flux, near_next
):
    nz, ny, _ = dims
    half = nz // 2
    even = is_even("tile")
    for z in range(nz):
        up = upward([tail[z, k : k + 1, :] for k in range(3)], tail[z + 1, 1:2, :])
        for q in range(2):
            near_next[z, q : q + 1, :] = jnp.where(even, up[q], head[z, q : q + 1, :])
    near_next[nz : nz + 3] = near_extra[...]
    hx_s, hy_s = flux.at[0], flux.at[1]
    ghost_flux(edged_reader(old_a, 0, head, tail, 0, ny), ghost, hx_s, hy_s, dims)

    def sweep(z, above):
        sweep_plane(
            edged_reader(old_a, z, head, tail, z, ny), above, reader(current, z), weight.at[z],
            writer(field, z), hx_s, hy_s, dims, False,
        )

    def plane(z, carry):
        sweep(z, edged_reader(old_a, z + 1, head, tail, z + 1, ny))
        return carry

    lax.fori_loop(0, half - 1, plane, 0)
    sweep(half - 1, edged_reader(old_b, 0, head, tail, half, ny))


def second_upper_kernel(dims, old, current, weight, flux, head, tail, field, flux_s):
    nz, ny, _ = dims
    half = nz // 2
    flux_s[...] = flux[...]

    def plane(z, carry):
        at = z + half
        sweep_plane(
            edged_reader(old, z, head, tail, at, ny), edged_reader(old, z + 1, head, tail, at + 1, ny),
            reader(current, z), weight.at[z], writer(field, z), flux_s.at[0], flux_s.at[1], dims, False,
        )
        return carry

    lax.fori_loop(0, nz - half, plane, 0)


def fix_trace_kernel(
    dims, field_a, field_b, weight_a, weight_b, near1, far1, head1, tail1, near, far,
    head, tail, traces, below, above,
):
    nz, ny, _ = dims
    half = nz // 2
    end = slice(ny - 1, ny)
    field = Planes(field_a, field_b, half, 1)
    weight = Planes(weight_a, weight_b, half, 0)
    low, high = halo_views(near, far)
    low1, high1 = halo_views(near1, far1)
    for side in range(2):
        z = (nz - 1) * side
        for k in range(2):
            traces[side, k] = field[k, z]
    for z in range(nz):
        head[z, 0:1, :], head[z, 1:2, :] = fixed_first(field, weight, low, z, z)
        x, y, zc = fixed_last(field, weight, high, z, z, ny)
        tail[z, 0:1, :], tail[z, 1:2, :], tail[z, 2:3, :] = x, y, zc
        if z in (0, nz - 1):
            side = 0 if z == 0 else 1
            traces[side, 0, 0:1, :] = head[z, 0:1, :]
            traces[side, 0, end, :] = x
            traces[side, 1, end, :] = y
    for side in range(2):
        z = (nz - 1) * side
        x, zc = head1[z, 0:1, :], head1[z, 1:2, :]
        rise = zc - head1[z - 1, 1:2, :] if z else zc
        w = low[nz + 2, side : side + 1, :]
        trace_low = (
            low[nz + side, 0:1, :] + w * x,
            low[nz + side, 1:2, :] - w * (rise + (x - row_prev(x))),
        )
        y = tail1[z, 1:2, :]
        w = high[nz + 2, side : side + 1, :]
        trace_high = (
            high[nz + side, 0:1, :] + w * (row_next(y) - y + tail1[z, 0:1, :]),
            high[nz + side, 1:2, :],
        )
        for k in range(2):
            for j in range(TERMS):
                at = side * TERMS + j
                below[at, k : k + 1, :] = trace_low[k] - pade_decays[j] * low1[nz + at, k : k + 1, :]
                above[at, k : k + 1, :] = trace_high[k] - pade_decays[j] * high1[nz + at, k : k + 1, :]


def surface_kernel(dims, traces, aux, below, above, fresh, even_side, odd_side, outgoing):
    _, ny, nx = dims
    rows, cols = ny // SUB, nx // LANE
    is_first_lane, is_last_lane, is_first_sub, is_last_sub = lane_masks()

    def part(side, carry):
        outgoing[side] = traces[side]

        def term(j, carry):
            decay = weight = F32(0.0)
            for q in range(TERMS):
                decay = jnp.where(j == q, F32(pade_decays[q]), decay)
                weight = jnp.where(j == q, F32(pade_weights[q]), weight)
            for k in range(2):

                def value(i, c):
                    r, s = tile_at(i, c)
                    return traces[side, k, r, s] - decay * aux[side, j, k, r, s]

                column = [value(i, 0) for i in range(rows)]
                lefts = [pltpu.roll(u, LANE - 1, 1) for u in column]
                rights = [0.0] * rows
                for c in range(cols):
                    ups = [pltpu.roll(u, SUB - 1, 0) for u in column]
                    downs = [pltpu.roll(u, 1, 0) for u in column]
                    after = [value(i, c + 1) for i in range(rows)] if c + 1 < cols else None
                    for i in range(rows):
                        r, s = tile_at(i, c)
                        u = column[i]
                        y_next = jnp.where(is_last_sub, ups[i + 1] if i + 1 < rows else 0.0, ups[i])
                        y_prev = jnp.where(is_first_sub, downs[i - 1] if i else 0.0, downs[i])
                        if after is not None:
                            beyond = pltpu.roll(after[i], LANE - 1, 1)
                        else:
                            beyond = u if k == 0 else 0.0
                        x_next = jnp.where(is_last_lane, beyond, lefts[i])
                        lefts[i] = beyond
                        right = pltpu.roll(u, 1, 1)
                        before = rights[i] if c else (u if k == 1 else 0.0)
                        x_prev = jnp.where(is_first_lane, before, right)
                        rights[i] = right
                        new = 0.5 * u - 0.125 * ((y_next + y_prev) + (x_next + x_prev))
                        fresh[side, j, k, r, s] = new
                        outgoing[side, k, r, s] += weight * new
                    column = after
            return carry

        return lax.fori_loop(0, TERMS, term, carry)

    lax.fori_loop(0, 2, part, 0)
    for side in range(2):
        for k in range(2):
            for source, r in ((below, slice(0, 1)), (above, slice(ny - 1, ny))):
                total = 0.0
                for j in range(TERMS):
                    total = total + (0.125 * pade_weights[j]) * source[side * TERMS + j, k : k + 1, :]
                outgoing[side, k, r, :] -= total
    even = is_even("slab")
    even_side[...] = jnp.where(even, outgoing[1], outgoing[0])
    odd_side[...] = jnp.where(even, outgoing[0], outgoing[1])


def write_kernel(dims, field_a, field_b, head, tail, smoothed, edges, sem):
    nz, ny, nx = dims
    half = nz // 2
    _, _, is_first_sub, is_last_sub = lane_masks()
    inner = pl.ds(SUB, ny - 2 * SUB)
    copies = []
    for n, (field, start, count) in enumerate(((field_a, 0, half), (field_b, half, nz - half))):
        planes = pl.ds(start, count)
        copies.append(pltpu.make_async_copy(field.at[:, :, inner], smoothed.at[:, planes, inner], sem.at[n]))
        copies[-1].start()
    for n, (field, start, count) in enumerate(((field_a, 0, half), (field_b, half, nz - half))):

        def merge(z, carry):
            at = z + start
            for c in range(nx // LANE):
                s = slice(c * LANE, (c + 1) * LANE)
                for k in range(3):
                    value = field[k, z, 0:SUB, s]
                    if k != 1:
                        value = jnp.where(is_first_sub, head[at, k // 2 : k // 2 + 1, s], value)
                    edges[0, k, at, :, s] = value
                    value = field[k, z, ny - SUB : ny, s]
                    edges[1, k, at, :, s] = jnp.where(is_last_sub, tail[at, k : k + 1, s], value)
            return carry

        lax.fori_loop(0, count, merge, 0)
        planes = pl.ds(start, count)
        for e, row in enumerate((0, ny - SUB)):
            copies.append(
                pltpu.make_async_copy(
                    edges.at[e, :, planes], smoothed.at[:, planes, pl.ds(row, SUB)], sem.at[2 + 2 * n + e]
                )
            )
            copies[-1].start()
    for copy in copies:
        copy.wait()


def faces_kernel(even_side, odd_side, out, sem):
    below = jnp.where(is_even("slab"), 0, 1)
    copies = [
        pltpu.make_async_copy(odd_side, out.at[0, below], sem.at[0]),
        pltpu.make_async_copy(even_side, out.at[0, 1 - below], sem.at[1]),
    ]
    for copy in copies:
        copy.start()
    for copy in copies:
        copy.wait()


def store_kernel(dims, fresh, low, high, out, edges, sem):
    _, ny, nx = dims
    inner = pl.ds(SUB, ny - 2 * SUB)
    middle = pltpu.make_async_copy(fresh.at[:, :, :, inner], out.at[0, :, :, :, inner], sem.at[0])
    middle.start()
    _, _, is_first_sub, is_last_sub = lane_masks()
    for side in range(2):
        for j in range(TERMS):
            for k in range(2):
                at = side * TERMS + j
                for c in range(nx // LANE):
                    s = slice(c * LANE, (c + 1) * LANE)
                    first = jnp.where(is_first_sub, 0.125 * low[at, k : k + 1, s], 0.0)
                    last = jnp.where(is_last_sub, 0.125 * high[at, k : k + 1, s], 0.0)
                    edges[0, side, j, k, :, s] = fresh[side, j, k, 0:SUB, s] - first
                    edges[1, side, j, k, :, s] = fresh[side, j, k, ny - SUB : ny, s] - last
    outer = [
        pltpu.make_async_copy(edges.at[e], out.at[0, :, :, :, pl.ds(start, SUB)], sem.at[1 + e])
        for e, start in enumerate((0, ny - SUB))
    ]
    for copy in outer:
        copy.start()
    middle.wait()
    for copy in outer:
        copy.wait()


def call(kernel, **options):
    return pl.pallas_call(kernel, **options)


def swap(block, axis, first):
    pairs = [(i, i + 1) for i in range(first, lax.axis_size(axis) - 1, 2)]
    return lax.ppermute(block, axis, [p for i, j in pairs for p in ((i, j), (j, i))])


def iteration(electric, current, mass, faces, aux):
    nz, ny, nx = mass.shape
    half = nz // 2
    dims = (nz, ny, nx)
    cells = nz * ny * nx
    bind = functools.partial
    rows1, rows2 = shape(nz + 2 * TERMS, 2, nx), shape(nz + 3, 2, nx)
    flux_shape = shape(2, ny, nx)
    dma = pltpu.SemaphoreType.DMA
    electric, current, mass, faces, aux = (
        pltpu.with_memory_space_constraint(a, pltpu.HBM) for a in (electric, current, mass, faces, aux)
    )
    aux_block = vm(2, TERMS, 2, SUB, nx)
    count = nz - half

    far1 = call(
        bind(pack_kernel, dims),
        out_shape=rows1,
        in_specs=[HBM] * 3,
        out_specs=VM,
        scratch_shapes=[vm(3, nz, SUB, nx), vm(SUB, nx), aux_block, dma((3,))],
        compiler_params=params(12),
    )(electric, faces, aux)
    far1 = swap(far1, "tile", 1)

    lower, current_a, weight_a, ghost, flux, near1 = call(
        bind(first_lower_kernel, dims),
        out_shape=(
            shape(3, half + 1, ny, nx),
            shape(3, half, ny, nx),
            shape(half, ny, nx),
            flux_shape,
            flux_shape,
            rows1,
        ),
        in_specs=[HBM] * 5,
        out_specs=(VM,) * 6,
        scratch_shapes=[vm(3, count, SUB, nx), vm(SUB, nx), aux_block]
        + [dma((half + 1,)), dma((half,)), dma((half,)), dma((4,))],
        compiler_params=params(16),
        cost_estimate=cost(25 * cells, 14 * cells),
    )(electric, current, mass, faces, aux)
    near1 = swap(near1, "tile", 0)

    upper, current_b, weight_b, aux_v = call(
        bind(first_upper_kernel, dims),
        out_shape=(
            shape(3, count + 1, ny, nx),
            shape(3, count, ny, nx),
            shape(count, ny, nx),
            shape(2, TERMS, 2, ny, nx),
        ),
        in_specs=[HBM] * 5 + [VM],
        out_specs=(VM,) * 4,
        scratch_shapes=[vm(2, ny, nx), dma((count,)), dma((count,)), dma((count,)), dma((3,))],
        compiler_params=params(16),
        cost_estimate=cost(25 * cells, 14 * cells),
    )(electric, current, mass, faces, aux, flux)

    heads, tails = shape(nz + 1, 2, nx), shape(nz + 1, 3, nx)
    head1, tail1, far2, near_extra = call(
        bind(fix_pack_kernel, dims),
        out_shape=(heads, tails, rows2, shape(3, 2, nx)),
        in_specs=[VM] * 9,
        out_specs=(VM,) * 4,
        compiler_params=params(12),
    )(lower, upper, current_a, current_b, weight_a, weight_b, ghost, near1, far1)
    far2 = swap(far2, "tile", 1)

    lower2, flux, near2 = call(
        bind(second_lower_kernel, dims),
        out_shape=(shape(3, half, ny, nx), flux_shape, rows2),
        in_specs=[VM] * 8,
        out_specs=(VM,) * 3,
        compiler_params=params(12),
        cost_estimate=cost(20 * cells, 14 * cells),
    )(lower, upper, current_a, weight_a, ghost, head1, tail1, near_extra)
    near2 = swap(near2, "tile", 0)

    upper2 = call(
        bind(second_upper_kernel, dims),
        out_shape=shape(3, count, ny, nx),
        in_specs=[VM] * 6,
        out_specs=VM,
        scratch_shapes=[vm(2, ny, nx)],
        compiler_params=params(12),
        cost_estimate=cost(20 * cells, 14 * cells),
    )(upper, current_b, weight_b, flux, head1, tail1)

    edge_rows = shape(2 * TERMS, 2, nx)
    head, tail, traces, below, above = call(
        bind(fix_trace_kernel, dims),
        out_shape=(heads, tails, shape(2, 2, ny, nx), edge_rows, edge_rows),
        in_specs=[VM] * 10,
        out_specs=(VM,) * 5,
        compiler_params=params(12),
    )(lower2, upper2, weight_a, weight_b, near1, far1, head1, tail1, near2, far2)

    side_shape = shape(2, ny, nx)
    fresh, even_side, odd_side = call(
        bind(surface_kernel, dims),
        out_shape=(shape(2, TERMS, 2, ny, nx), side_shape, side_shape),
        in_specs=[VM] * 4,
        out_specs=(VM,) * 3,
        scratch_shapes=[vm(2, 2, ny, nx)],
        compiler_params=params(12),
        cost_estimate=cost(20 * 16 * ny * nx, 12 * cells),
    )(traces, aux_v, below, above)
    odd_side = swap(odd_side, "slab", 1)
    even_side = swap(even_side, "slab", 0)

    smoothed = call(
        bind(write_kernel, dims),
        out_shape=shape(3, nz, ny, nx),
        in_specs=[VM] * 4,
        out_specs=HBM,
        scratch_shapes=[vm(2, 3, nz, SUB, nx), dma((6,))],
        compiler_params=params(12),
        cost_estimate=cost(cells, 12 * cells),
    )(lower2, upper2, head, tail)

    fresh = call(
        bind(store_kernel, dims),
        out_shape=shape(1, 2, TERMS, 2, ny, nx),
        in_specs=[VM] * 3,
        out_specs=HBM,
        scratch_shapes=[vm(2, 2, TERMS, 2, SUB, nx), dma((3,))],
        compiler_params=params(8),
        cost_estimate=cost(16 * ny * nx, 8 * 16 * ny * nx),
    )(fresh, below, above)

    next_faces = call(
        faces_kernel,
        out_shape=shape(1, 2, 2, ny, nx),
        in_specs=[VM] * 2,
        out_specs=HBM,
        scratch_shapes=[dma((2,))],
        compiler_params=params(8),
    )(even_side, odd_side)
    return smoothed, next_faces, fresh


def solution(mesh):
    placed = (
        P(None, "slab", "tile", None),
        P(None, "slab", "tile", None),
        P("slab", "tile", None),
        P("slab", None, None, "tile", None),
        P("slab", None, None, None, "tile", None),
    )
    return jax.shard_map(
        iteration,
        mesh=mesh,
        in_specs=placed,
        out_specs=(
            P(None, "slab", "tile", None),
            P("slab", None, None, "tile", None),
            P("slab", None, None, None, "tile", None),
        ),
        check_vma=False,
    )
```

```python
import functools
import math

import jax
import jax.numpy as jnp
from jax import lax
from jax.experimental import pallas as pl
from jax.experimental.pallas import tpu as pltpu
from jax.sharding import PartitionSpec as P


pade_weights = [2.0 / 9.0 * math.sin(j * math.pi / 9.0) ** 2 for j in range(1, 5)]
pade_decays = [math.cos(j * math.pi / 9.0) ** 2 for j in range(1, 5)]
TERMS = 4
SUB, LANE = 8, 128
F32 = jnp.float32
HBM = pl.BlockSpec(memory_space=pltpu.HBM)
VM = pl.BlockSpec(memory_space=pltpu.VMEM)


def params(mib):
    return pltpu.CompilerParams(vmem_limit_bytes=mib << 20)


def shape(*dims):
    return jax.ShapeDtypeStruct(dims, F32)


def cost(flops, count):
    return pl.CostEstimate(flops=flops, bytes_accessed=count, transcendentals=0)


def vm(*dims):
    return pltpu.VMEM(dims, F32)


def row_next(row):
    n = row.shape[1]
    at = lax.broadcasted_iota(jnp.int32, row.shape, 1)
    return jnp.where(at == n - 1, 0.0, pltpu.roll(row, n - 1, 1))


def row_prev(row):
    at = lax.broadcasted_iota(jnp.int32, row.shape, 1)
    return jnp.where(at == 0, 0.0, pltpu.roll(row, 1, 1))


def is_even(axis):
    return lax.rem(lax.axis_index(axis), 2) == 0


class Either:
    def __init__(self, choose, first, second):
        self.choose, self.first, self.second = choose, first, second

    def __getitem__(self, at):
        return jnp.where(self.choose, self.first[at], self.second[at])


def halo_views(near, far):
    even = is_even("tile")
    return Either(even, far, near), Either(even, near, far)


def upward(last, y_above):
    x, y, z = last
    return row_next(y) - y + x, z + (y_above - y)


def fixed_first(field, weight, low, z, zz):
    w = weight[z, 0:1, :]
    return field[0, zz, 0:1, :] + w * low[z, 0:1, :], field[2, zz, 0:1, :] + w * low[z, 1:2, :]


def fixed_last(field, weight, high, z, zz, ny):
    end = slice(ny - 1, ny)
    w = weight[z, end, :]
    hx, hz = high[z, 0:1, :], high[z, 1:2, :]
    rise = hz - high[z - 1, 1:2, :] if z else hz
    return (
        field[0, zz, end, :] + w * hx,
        field[1, zz, end, :] - w * (rise + (hx - row_prev(hx))),
        field[2, zz, end, :] + w * hz,
    )


def lane_masks():
    lane = lax.broadcasted_iota(jnp.int32, (SUB, LANE), 1)
    sub = lax.broadcasted_iota(jnp.int32, (SUB, LANE), 0)
    return lane == 0, lane == LANE - 1, sub == 0, sub == SUB - 1


def tile_at(i, c):
    return slice(i * SUB, (i + 1) * SUB), slice(c * LANE, (c + 1) * LANE)


def pack_kernel(dims, electric, faces, aux, far, block, top, aux_block, sem):
    nz, ny, _ = dims
    even = is_even("tile")
    start = pl.multiple_of(jnp.where(even, 0, ny - SUB), SUB)
    copies = [
        pltpu.make_async_copy(electric.at[:, :, pl.ds(start, SUB)], block, sem.at[0]),
        pltpu.make_async_copy(faces.at[0, 1, 1, pl.ds(ny - SUB, SUB)], top, sem.at[1]),
        pltpu.make_async_copy(aux.at[0, :, :, :, pl.ds(start, SUB)], aux_block, sem.at[2]),
    ]
    for copy in copies:
        copy.start()
    for copy in copies:
        copy.wait()
    end = slice(SUB - 1, SUB)
    for z in range(nz):
        y_above = block[1, z + 1, end, :] if z + 1 < nz else top[end, :]
        up = upward([block[k, z, end, :] for k in range(3)], y_above)
        for q in range(2):
            far[z, q : q + 1, :] = jnp.where(even, block[2 * q, z, 0:1, :], up[q])
    for side in range(2):
        for j in range(TERMS):
            for k in range(2):
                far[nz + side * TERMS + j, k : k + 1, :] = jnp.where(
                    even, aux_block[side, j, k, 0:1, :], aux_block[side, j, k, end, :]
                )


def sweep_plane(load, above, current, weight, store, hx_s, hy_s, dims, from_mass):
    _, ny, nx = dims
    rows, cols = ny // SUB, nx // LANE
    is_first_lane, is_last_lane, is_first_sub, is_last_sub = lane_masks()

    def left(k, i, c):
        return pltpu.roll(load(k, i, c), LANE - 1, 1)

    lefts = {(k, i): left(k, i, 0) for k in (1, 2) for i in range(rows)}
    right_y, right_z = {}, {}
    for c in range(cols):
        here = [[load(k, i, c) for k in range(3)] for i in range(rows)]
        ups = [{k: pltpu.roll(here[i][k], SUB - 1, 0) for k in (0, 2)} for i in range(rows)]
        down_x = down_z = None
        for i in range(rows):
            r, s = tile_at(i, c)

            def y_next(k):
                return jnp.where(is_last_sub, ups[i + 1][k] if i + 1 < rows else 0.0, ups[i][k])

            def x_next(k):
                after = left(k, i, c + 1) if c + 1 < cols else 0.0
                value = jnp.where(is_last_lane, after, lefts[k, i])
                lefts[k, i] = after
                return value

            ex, ey, ez = here[i]
            hx = (y_next(2) - ez) - (above(1, i, c) - ey)
            hy = (above(0, i, c) - ex) - (x_next(2) - ez)
            hz = (x_next(1) - ey) - (y_next(0) - ex)
            hx_low, hy_low = hx_s[r, s], hy_s[r, s]
            hx_s[r, s] = hx
            hy_s[r, s] = hy
            dx = pltpu.roll(hx, 1, 0)
            dz = pltpu.roll(hz, 1, 0)
            hx_y = jnp.where(is_first_sub, ez if i == 0 else down_x, dx)
            hz_y = jnp.where(is_first_sub, -ex if i == 0 else down_z, dz)
            down_x, down_z = dx, dz
            ry = pltpu.roll(hy, 1, 1)
            rz = pltpu.roll(hz, 1, 1)
            hy_x = jnp.where(is_first_lane, 0.0 if c == 0 else right_y[i], ry)
            hz_x = jnp.where(is_first_lane, 0.0 if c == 0 else right_z[i], rz)
            right_y[i], right_z[i] = ry, rz
            cx = (hz - hz_y) - (hy - hy_low)
            cy = (hx - hx_low) - (hz - hz_x)
            cz = (hy - hy_x) - (hx - hx_y)
            w = weight[r, s]
            if from_mass:
                w = 0.5 / (w + 4.0)
                weight[r, s] = w
            keep = 4.0 * w + 0.5
            store(0, i, c, keep * ex + w * (current(0, i, c) - cx))
            store(1, i, c, keep * ey + w * (current(1, i, c) - cy))
            store(2, i, c, keep * ez + w * (current(2, i, c) - cz))


def reader(ref, z):
    def load(k, i, c):
        r, s = tile_at(i, c)
        return ref[k, z, r, s]

    return load


def writer(ref, z):
    def store(k, i, c, value):
        r, s = tile_at(i, c)
        ref[k, z, r, s] = value

    return store


def ghost_flux(load, ghost, hx_s, hy_s, dims):
    _, ny, nx = dims
    for i in range(ny // SUB):
        for c in range(nx // LANE):
            r, s = tile_at(i, c)
            hx_s[r, s] = ghost[1, r, s] - load(1, i, c)
            hy_s[r, s] = load(0, i, c) - ghost[0, r, s]


def first_lower_kernel(
    dims, electric, current_h, mass, faces, aux_h,
    field, current, weight, ghost, flux, near,
    block, top, aux_block, field_sem, current_sem, weight_sem, sem,
):
    nz, ny, _ = dims
    half = nz // 2
    even = is_even("tile")
    end = slice(ny - 1, ny)
    tile_end = slice(SUB - 1, SUB)
    copy = pltpu.make_async_copy
    row = pl.multiple_of(jnp.where(even, ny - SUB, 0), SUB)

    def field_copy(z):
        return copy(electric.at[:, pl.ds(z, 1)], field.at[:, pl.ds(z, 1)], field_sem.at[z])

    def current_copy(z):
        return copy(current_h.at[:, pl.ds(z, 1)], current.at[:, pl.ds(z, 1)], current_sem.at[z])

    def weight_copy(z):
        return copy(mass.at[pl.ds(z, 1)], weight.at[pl.ds(z, 1)], weight_sem.at[z])

    low_copy = copy(faces.at[0, 0], ghost, sem.at[0])
    edge_copies = [
        copy(electric.at[:, pl.ds(half, nz - half), pl.ds(row, SUB)], block, sem.at[1]),
        copy(faces.at[0, 1, 1, pl.ds(ny - SUB, SUB)], top, sem.at[2]),
        copy(aux_h.at[0, :, :, :, pl.ds(row, SUB)], aux_block, sem.at[3]),
    ]
    low_copy.start()
    field_copy(0).start()

    def start(z, carry):
        field_copy(z + 1).start()
        current_copy(z).start()
        weight_copy(z).start()
        return carry

    lax.fori_loop(0, half, start, 0)
    for edge in edge_copies:
        edge.start()

    low_copy.wait()
    field_copy(0).wait()
    hx_s, hy_s = flux.at[0], flux.at[1]
    ghost_flux(reader(field, 0), ghost, hx_s, hy_s, dims)

    def plane(z, carry):
        field_copy(z + 1).wait()
        up = upward([field[k, z, end, :] for k in range(3)], field[1, z + 1, end, :])
        for q in range(2):
            near[z, q : q + 1, :] = jnp.where(even, up[q], field[2 * q, z, 0:1, :])
        current_copy(z).wait()
        weight_copy(z).wait()
        sweep_plane(
            reader(field, z), reader(field, z + 1), reader(current, z), weight.at[z], writer(field, z), hx_s, hy_s, dims, True
        )
        return carry

    lax.fori_loop(0, half, plane, 0)
    for edge in edge_copies:
        edge.wait()
    for z in range(nz - half):
        y_above = block[1, z + 1, tile_end, :] if z + 1 < nz - half else top[tile_end, :]
        up = upward([block[k, z, tile_end, :] for k in range(3)], y_above)
        for q in range(2):
            near[half + z, q : q + 1, :] = jnp.where(even, up[q], block[2 * q, z, 0:1, :])
    for side in range(2):
        for j in range(TERMS):
            for k in range(2):
                near[nz + side * TERMS + j, k : k + 1, :] = jnp.where(
                    even, aux_block[side, j, k, tile_end, :], aux_block[side, j, k, 0:1, :]
                )


def first_upper_kernel(
    dims, electric, current_h, mass, faces, aux_h, flux,
    field, current, weight, aux,
    flux_s, field_sem, current_sem, weight_sem, sem,
):
    nz, _, _ = dims
    half = nz // 2
    count = nz - half
    copy = pltpu.make_async_copy

    def field_copy(z):
        return copy(electric.at[:, pl.ds(z + half, 1)], field.at[:, pl.ds(z, 1)], field_sem.at[z])

    def current_copy(z):
        return copy(current_h.at[:, pl.ds(z + half, 1)], current.at[:, pl.ds(z, 1)], current_sem.at[z])

    def weight_copy(z):
        return copy(mass.at[pl.ds(z + half, 1)], weight.at[pl.ds(z, 1)], weight_sem.at[z])

    high_copies = [copy(faces.at[0, 1, k], field.at[k, count], sem.at[k]) for k in range(2)]
    aux_copy = copy(aux_h.at[0], aux, sem.at[2])
    field_copy(0).start()

    def start(z, carry):
        field_copy(z + 1).start()
        current_copy(z).start()
        weight_copy(z).start()
        return carry

    lax.fori_loop(0, count - 1, start, 0)
    current_copy(count - 1).start()
    weight_copy(count - 1).start()
    for high in high_copies:
        high.start()
    aux_copy.start()
    flux_s[...] = flux[...]
    field_copy(0).wait()

    def plane(z, carry):
        @pl.when(z + 1 < count)
        def _():
            field_copy(z + 1).wait()

        @pl.when(z + 1 == count)
        def _():
            for high in high_copies:
                high.wait()

        current_copy(z).wait()
        weight_copy(z).wait()
        sweep_plane(
            reader(field, z), reader(field, z + 1), reader(current, z),
            weight.at[z], writer(field, z), flux_s.at[0], flux_s.at[1], dims, True,
        )
        return carry

    lax.fori_loop(0, count, plane, 0)
    aux_copy.wait()


class Planes:
    def __init__(self, lower, upper, half, dim):
        self.lower, self.upper, self.half, self.dim = lower, upper, half, dim

    def __getitem__(self, at):
        z = at[self.dim]
        if z < self.half:
            return self.lower[at]
        return self.upper[at[: self.dim] + (z - self.half,) + at[self.dim + 1 :]]


def fix_pack_kernel(
    dims, field_a, field_b, current_a, current_b, weight_a, weight_b, ghost, near, far,
    head, tail, far_next, near_extra,
):
    nz, ny, nx = dims
    half = nz // 2
    even = is_even("tile")
    end = slice(ny - 1, ny)
    field = Planes(field_a, field_b, half, 1)
    current = Planes(current_a, current_b, half, 1)
    weight = Planes(weight_a, weight_b, half, 0)
    low, high = halo_views(near, far)
    for z in range(nz):
        head[z, 0:1, :], head[z, 1:2, :] = fixed_first(field, weight, low, z, z)
        x, y, zc = fixed_last(field, weight, high, z, z, ny)
        tail[z, 0:1, :], tail[z, 1:2, :], tail[z, 2:3, :] = x, y, zc
    head[nz, 0:1, :] = field[0, nz, 0:1, :]
    tail[nz, 0:1, :] = field[0, nz, end, :]
    tail[nz, 1:2, :] = field[1, nz, end, :]
    for z in range(nz):
        up = upward([tail[z, k : k + 1, :] for k in range(3)], tail[z + 1, 1:2, :])
        for q in range(2):
            far_next[z, q : q + 1, :] = jnp.where(even, head[z, q : q + 1, :], up[q])

    def value(k, z, r):
        at = slice(r, r + 1)
        if r in (-1, ny) or (k == 2 and z in (-1, nz)):
            return jnp.zeros((1, nx), F32)
        if z == -1:
            return ghost[k, at, :]
        if r == 0 and k != 1:
            return head[z, k // 2 : k // 2 + 1, :]
        if r == ny - 1:
            return tail[z, k : k + 1, :]
        return field[k, z, at, :]

    def flux_x(z, r):
        return (value(2, z, r + 1) - value(2, z, r)) - (value(1, z + 1, r) - value(1, z, r))

    def flux_y(z, r):
        here = value(2, z, r)
        return (value(0, z + 1, r) - value(0, z, r)) - (row_next(here) - here)

    def flux_z(z, r):
        here = value(1, z, r)
        return (row_next(here) - here) - (value(0, z, r + 1) - value(0, z, r))

    def trace(z, r):
        at = slice(r, r + 1)
        hz = flux_z(z, r)
        cx = (hz - flux_z(z, r - 1)) - (flux_y(z, r) - flux_y(z - 1, r))
        cy = (flux_x(z, r) - flux_x(z - 1, r)) - (hz - row_prev(hz))
        w = weight[z, at, :]
        keep = 4.0 * w + 0.5
        return (
            keep * value(0, z, r) + w * (current[0, z, at, :] - cx),
            keep * value(1, z, r) + w * (current[1, z, at, :] - cy),
            w,
        )

    for side in range(2):
        z = (nz - 1) * side
        down, up = trace(z, 0), trace(z, ny - 1)
        for k in range(2):
            far_next[nz + side, k : k + 1, :] = jnp.where(even, down[k], up[k])
            near_extra[side, k : k + 1, :] = jnp.where(even, up[k], down[k])
        far_next[nz + 2, side : side + 1, :] = jnp.where(even, down[2], up[2])
        near_extra[2, side : side + 1, :] = jnp.where(even, up[2], down[2])


def edged_reader(ref, z, head, tail, plane, ny):
    rows = ny // SUB
    _, _, is_first_sub, is_last_sub = lane_masks()

    def load(k, i, c):
        r, s = tile_at(i, c)
        value = ref[k, z, r, s]
        if i == 0 and k != 1:
            value = jnp.where(is_first_sub, head[plane, k // 2 : k // 2 + 1, s], value)
        if i == rows - 1:
            value = jnp.where(is_last_sub, tail[plane, k : k + 1, s], value)
        return value

    return load


def second_lower_kernel(
    dims, old_a, old_b, current, weight, ghost, head, tail, near_extra, field, flux, near_next
):
    nz, ny, _ = dims
    half = nz // 2
    even = is_even("tile")
    for z in range(nz):
        up = upward([tail[z, k : k + 1, :] for k in range(3)], tail[z + 1, 1:2, :])
        for q in range(2):
            near_next[z, q : q + 1, :] = jnp.where(even, up[q], head[z, q : q + 1, :])
    near_next[nz : nz + 3] = near_extra[...]
    hx_s, hy_s = flux.at[0], flux.at[1]
    ghost_flux(edged_reader(old_a, 0, head, tail, 0, ny), ghost, hx_s, hy_s, dims)

    def sweep(z, above):
        sweep_plane(
            edged_reader(old_a, z, head, tail, z, ny), above, reader(current, z), weight.at[z],
            writer(field, z), hx_s, hy_s, dims, False,
        )

    def plane(z, carry):
        sweep(z, edged_reader(old_a, z + 1, head, tail, z + 1, ny))
        return carry

    lax.fori_loop(0, half - 1, plane, 0)
    sweep(half - 1, edged_reader(old_b, 0, head, tail, half, ny))


def inner_copies(field, smoothed, sem, start, z, count, ny):
    inner = pl.ds(SUB, ny - 2 * SUB)
    return pltpu.make_async_copy(
        field.at[:, pl.ds(z, count), inner], smoothed.at[:, pl.ds(start + z, count), inner], sem
    )


LATE = 2


def second_upper_kernel(
    dims, old, current, weight, flux, head, tail, lower, field, smoothed, flux_s, sem
):
    nz, ny, _ = dims
    half = nz // 2
    count = nz - half
    early = inner_copies(lower, smoothed, sem.at[count], 0, 0, half, ny)
    early.start()
    flux_s[...] = flux[...]

    def out(z):
        return inner_copies(field, smoothed, sem.at[z], half, z, 1, ny)

    def plane(z, carry):
        at = z + half
        sweep_plane(
            edged_reader(old, z, head, tail, at, ny), edged_reader(old, z + 1, head, tail, at + 1, ny),
            reader(current, z), weight.at[z], writer(field, z), flux_s.at[0], flux_s.at[1], dims, False,
        )

        @pl.when(z < count - LATE)
        def _():
            out(z).start()

        return carry

    lax.fori_loop(0, count, plane, 0)
    for z in range(count - LATE):
        out(z).wait()
    early.wait()


def fix_trace_kernel(
    dims, field_a, field_b, weight_a, weight_b, near1, far1, head1, tail1, near, far,
    head, tail, traces, below, above,
):
    nz, ny, _ = dims
    half = nz // 2
    end = slice(ny - 1, ny)
    field = Planes(field_a, field_b, half, 1)
    weight = Planes(weight_a, weight_b, half, 0)
    low, high = halo_views(near, far)
    low1, high1 = halo_views(near1, far1)
    for side in range(2):
        z = (nz - 1) * side
        for k in range(2):
            traces[side, k] = field[k, z]
    for z in range(nz):
        head[z, 0:1, :], head[z, 1:2, :] = fixed_first(field, weight, low, z, z)
        x, y, zc = fixed_last(field, weight, high, z, z, ny)
        tail[z, 0:1, :], tail[z, 1:2, :], tail[z, 2:3, :] = x, y, zc
        if z in (0, nz - 1):
            side = 0 if z == 0 else 1
            traces[side, 0, 0:1, :] = head[z, 0:1, :]
            traces[side, 0, end, :] = x
            traces[side, 1, end, :] = y
    for side in range(2):
        z = (nz - 1) * side
        x, zc = head1[z, 0:1, :], head1[z, 1:2, :]
        rise = zc - head1[z - 1, 1:2, :] if z else zc
        w = low[nz + 2, side : side + 1, :]
        trace_low = (
            low[nz + side, 0:1, :] + w * x,
            low[nz + side, 1:2, :] - w * (rise + (x - row_prev(x))),
        )
        y = tail1[z, 1:2, :]
        w = high[nz + 2, side : side + 1, :]
        trace_high = (
            high[nz + side, 0:1, :] + w * (row_next(y) - y + tail1[z, 0:1, :]),
            high[nz + side, 1:2, :],
        )
        for k in range(2):
            for j in range(TERMS):
                at = side * TERMS + j
                below[at, k : k + 1, :] = trace_low[k] - pade_decays[j] * low1[nz + at, k : k + 1, :]
                above[at, k : k + 1, :] = trace_high[k] - pade_decays[j] * high1[nz + at, k : k + 1, :]


def surface_tiles(dims, k, value, edge_low, edge_high, emit):
    _, ny, nx = dims
    rows, cols = ny // SUB, nx // LANE
    is_first_lane, is_last_lane, is_first_sub, is_last_sub = lane_masks()
    column = [value(i, 0) for i in range(rows)]
    lefts = [pltpu.roll(u, LANE - 1, 1) for u in column]
    rights = [0.0] * rows
    for c in range(cols):
        s = slice(c * LANE, (c + 1) * LANE)
        ups = [pltpu.roll(u, SUB - 1, 0) for u in column] + [edge_high(s)]
        downs = [edge_low(s)] + [pltpu.roll(u, 1, 0) for u in column]
        after = [value(i, c + 1) for i in range(rows)] if c + 1 < cols else None
        for i in range(rows):
            u = column[i]
            y_next = jnp.where(is_last_sub, ups[i + 1], ups[i])
            y_prev = jnp.where(is_first_sub, downs[i], downs[i + 1])
            if after is not None:
                beyond = pltpu.roll(after[i], LANE - 1, 1)
            else:
                beyond = u if k == 0 else 0.0
            x_next = jnp.where(is_last_lane, beyond, lefts[i])
            lefts[i] = beyond
            right = pltpu.roll(u, 1, 1)
            before = rights[i] if c else (u if k == 1 else 0.0)
            x_prev = jnp.where(is_first_lane, before, right)
            rights[i] = right
            emit(i, c, 0.5 * u - 0.125 * ((y_next + y_prev) + (x_next + x_prev)))
        column = after


def outgoing_kernel(dims, traces, aux, below, above, even_side, odd_side):
    even = is_even("slab")
    total = sum(pade_weights)
    for out, side in ((even_side, jnp.where(even, 1, 0)), (odd_side, jnp.where(even, 0, 1))):
        for k in range(2):

            def value(i, c):
                r, s = tile_at(i, c)
                u = total * traces[side, k, r, s]
                for j in range(TERMS):
                    u = u - (pade_weights[j] * pade_decays[j]) * aux[side, j, k, r, s]
                return u

            def edge(source):
                def row(s):
                    u = 0.0
                    for j in range(TERMS):
                        u = u + pade_weights[j] * source[side * TERMS + j, k : k + 1, s]
                    return u

                return row

            def emit(i, c, new):
                r, s = tile_at(i, c)
                out[k, r, s] = traces[side, k, r, s] + new

            surface_tiles(dims, k, value, edge(below), edge(above), emit)


def surface_kernel(dims, traces, aux, below, above, out, fresh, sem):
    def copy(side, j):
        return pltpu.make_async_copy(fresh.at[side, j], out.at[0, side, j], sem.at[side * TERMS + j])

    def term(at, carry):
        side, j = at // TERMS, at % TERMS
        decay = F32(0.0)
        for q in range(TERMS):
            decay = jnp.where(j == q, F32(pade_decays[q]), decay)
        for k in range(2):

            def value(i, c):
                r, s = tile_at(i, c)
                return traces[side, k, r, s] - decay * aux[side, j, k, r, s]

            def emit(i, c, new):
                r, s = tile_at(i, c)
                fresh[side, j, k, r, s] = new

            surface_tiles(
                dims, k, value, lambda s: below[at, k : k + 1, s], lambda s: above[at, k : k + 1, s], emit
            )
        copy(side, j).start()
        return carry

    lax.fori_loop(0, 2 * TERMS, term, 0)
    for side in range(2):
        for j in range(TERMS):
            copy(side, j).wait()


def write_kernel(dims, field_a, field_b, head, tail, old, smoothed, edges, sem):
    nz, ny, nx = dims
    half = nz // 2
    count = nz - half
    _, _, is_first_sub, is_last_sub = lane_masks()
    copies = [inner_copies(field_b, smoothed, sem.at[0], half, count - LATE, LATE, ny)]
    copies[0].start()
    for n, (field, start, planes) in enumerate(((field_a, 0, half), (field_b, half, count))):

        def merge(z, carry):
            at = z + start
            for c in range(nx // LANE):
                s = slice(c * LANE, (c + 1) * LANE)
                for k in range(3):
                    value = field[k, z, 0:SUB, s]
                    if k != 1:
                        value = jnp.where(is_first_sub, head[at, k // 2 : k // 2 + 1, s], value)
                    edges[0, k, at, :, s] = value
                    value = field[k, z, ny - SUB : ny, s]
                    edges[1, k, at, :, s] = jnp.where(is_last_sub, tail[at, k : k + 1, s], value)
            return carry

        lax.fori_loop(0, planes, merge, 0)
        span = pl.ds(start, planes)
        for e, row in enumerate((0, ny - SUB)):
            copies.append(
                pltpu.make_async_copy(
                    edges.at[e, :, span], smoothed.at[:, span, pl.ds(row, SUB)], sem.at[1 + 2 * n + e]
                )
            )
            copies[-1].start()
    for copy in copies:
        copy.wait()


def faces_kernel(even_side, odd_side, out, sem):
    below = jnp.where(is_even("slab"), 0, 1)
    copies = [
        pltpu.make_async_copy(odd_side, out.at[0, below], sem.at[0]),
        pltpu.make_async_copy(even_side, out.at[0, 1 - below], sem.at[1]),
    ]
    for copy in copies:
        copy.start()
    for copy in copies:
        copy.wait()


def call(kernel, **options):
    return pl.pallas_call(kernel, **options)


def swap(block, axis, first):
    pairs = [(i, i + 1) for i in range(first, lax.axis_size(axis) - 1, 2)]
    return lax.ppermute(block, axis, [p for i, j in pairs for p in ((i, j), (j, i))])


def iteration(electric, current, mass, faces, aux):
    nz, ny, nx = mass.shape
    half = nz // 2
    dims = (nz, ny, nx)
    cells = nz * ny * nx
    bind = functools.partial
    rows1, rows2 = shape(nz + 2 * TERMS, 2, nx), shape(nz + 3, 2, nx)
    flux_shape = shape(2, ny, nx)
    dma = pltpu.SemaphoreType.DMA
    electric, current, mass, faces, aux = (
        pltpu.with_memory_space_constraint(a, pltpu.HBM) for a in (electric, current, mass, faces, aux)
    )
    aux_block = vm(2, TERMS, 2, SUB, nx)
    count = nz - half

    far1 = call(
        bind(pack_kernel, dims),
        out_shape=rows1,
        in_specs=[HBM] * 3,
        out_specs=VM,
        scratch_shapes=[vm(3, nz, SUB, nx), vm(SUB, nx), aux_block, dma((3,))],
        compiler_params=params(12),
    )(electric, faces, aux)
    far1 = swap(far1, "tile", 1)

    lower, current_a, weight_a, ghost, flux, near1 = call(
        bind(first_lower_kernel, dims),
        out_shape=(
            shape(3, half + 1, ny, nx),
            shape(3, half, ny, nx),
            shape(half, ny, nx),
            flux_shape,
            flux_shape,
            rows1,
        ),
        in_specs=[HBM] * 5,
        out_specs=(VM,) * 6,
        scratch_shapes=[vm(3, count, SUB, nx), vm(SUB, nx), aux_block]
        + [dma((half + 1,)), dma((half,)), dma((half,)), dma((4,))],
        compiler_params=params(16),
        cost_estimate=cost(25 * cells, 14 * cells),
    )(electric, current, mass, faces, aux)
    near1 = swap(near1, "tile", 0)

    upper, current_b, weight_b, aux_v = call(
        bind(first_upper_kernel, dims),
        out_shape=(
            shape(3, count + 1, ny, nx),
            shape(3, count, ny, nx),
            shape(count, ny, nx),
            shape(2, TERMS, 2, ny, nx),
        ),
        in_specs=[HBM] * 5 + [VM],
        out_specs=(VM,) * 4,
        scratch_shapes=[vm(2, ny, nx), dma((count,)), dma((count,)), dma((count,)), dma((3,))],
        compiler_params=params(16),
        cost_estimate=cost(25 * cells, 14 * cells),
    )(electric, current, mass, faces, aux, flux)

    heads, tails = shape(nz + 1, 2, nx), shape(nz + 1, 3, nx)
    head1, tail1, far2, near_extra = call(
        bind(fix_pack_kernel, dims),
        out_shape=(heads, tails, rows2, shape(3, 2, nx)),
        in_specs=[VM] * 9,
        out_specs=(VM,) * 4,
        compiler_params=params(12),
    )(lower, upper, current_a, current_b, weight_a, weight_b, ghost, near1, far1)
    far2 = swap(far2, "tile", 1)

    lower2, flux, near2 = call(
        bind(second_lower_kernel, dims),
        out_shape=(shape(3, half, ny, nx), flux_shape, rows2),
        in_specs=[VM] * 8,
        out_specs=(VM,) * 3,
        compiler_params=params(12),
        cost_estimate=cost(20 * cells, 14 * cells),
    )(lower, upper, current_a, weight_a, ghost, head1, tail1, near_extra)
    near2 = swap(near2, "tile", 0)

    upper2, smoothed = call(
        bind(second_upper_kernel, dims),
        out_shape=(shape(3, count, ny, nx), shape(3, nz, ny, nx)),
        in_specs=[VM] * 7,
        out_specs=(VM, HBM),
        scratch_shapes=[vm(2, ny, nx), dma((count + 1,))],
        compiler_params=params(12),
        cost_estimate=cost(20 * cells, 14 * cells),
    )(upper, current_b, weight_b, flux, head1, tail1, lower2)

    edge_rows = shape(2 * TERMS, 2, nx)
    head, tail, traces, below, above = call(
        bind(fix_trace_kernel, dims),
        out_shape=(heads, tails, shape(2, 2, ny, nx), edge_rows, edge_rows),
        in_specs=[VM] * 10,
        out_specs=(VM,) * 5,
        compiler_params=params(12),
    )(lower2, upper2, weight_a, weight_b, near1, far1, head1, tail1, near2, far2)

    even_side, odd_side = call(
        bind(outgoing_kernel, dims),
        out_shape=(flux_shape, flux_shape),
        in_specs=[VM] * 4,
        out_specs=(VM,) * 2,
        compiler_params=params(8),
    )(traces, aux_v, below, above)
    odd_side = swap(odd_side, "slab", 1)
    even_side = swap(even_side, "slab", 0)

    fresh = call(
        bind(surface_kernel, dims),
        out_shape=shape(1, 2, TERMS, 2, ny, nx),
        in_specs=[VM] * 4,
        out_specs=HBM,
        scratch_shapes=[vm(2, TERMS, 2, ny, nx), dma((2 * TERMS,))],
        compiler_params=params(8),
        cost_estimate=cost(12 * 16 * ny * nx, 12 * 16 * ny * nx),
    )(traces, aux_v, below, above)

    smoothed = call(
        bind(write_kernel, dims),
        out_shape=shape(3, nz, ny, nx),
        in_specs=[VM] * 4 + [HBM],
        out_specs=HBM,
        input_output_aliases={4: 0},
        scratch_shapes=[vm(2, 3, nz, SUB, nx), dma((5,))],
        compiler_params=params(12),
        cost_estimate=cost(cells, 12 * cells),
    )(lower2, upper2, head, tail, smoothed)

    next_faces = call(
        faces_kernel,
        out_shape=shape(1, 2, 2, ny, nx),
        in_specs=[VM] * 2,
        out_specs=HBM,
        scratch_shapes=[dma((2,))],
        compiler_params=params(8),
    )(even_side, odd_side)
    return smoothed, next_faces, fresh


def solution(mesh):
    placed = (
        P(None, "slab", "tile", None),
        P(None, "slab", "tile", None),
        P("slab", "tile", None),
        P("slab", None, None, "tile", None),
        P("slab", None, None, None, "tile", None),
    )
    return jax.shard_map(
        iteration,
        mesh=mesh,
        in_specs=placed,
        out_specs=(
            P(None, "slab", "tile", None),
            P("slab", None, None, "tile", None),
            P("slab", None, None, None, "tile", None),
        ),
        check_vma=False,
    )
```

```python
import functools
import math

import jax
import jax.numpy as jnp
from jax import lax
from jax.experimental import pallas as pl
from jax.experimental.pallas import tpu as pltpu
from jax.sharding import PartitionSpec as P


pade_weights = [2.0 / 9.0 * math.sin(j * math.pi / 9.0) ** 2 for j in range(1, 5)]
pade_decays = [math.cos(j * math.pi / 9.0) ** 2 for j in range(1, 5)]
TERMS = 4
SUB, LANE = 8, 128
F32 = jnp.float32
HBM = pl.BlockSpec(memory_space=pltpu.HBM)
VM = pl.BlockSpec(memory_space=pltpu.VMEM)


def params(mib):
    return pltpu.CompilerParams(vmem_limit_bytes=mib << 20)


def shape(*dims):
    return jax.ShapeDtypeStruct(dims, F32)


def cost(flops, count):
    return pl.CostEstimate(flops=flops, bytes_accessed=count, transcendentals=0)


def vm(*dims):
    return pltpu.VMEM(dims, F32)


def row_next(row):
    n = row.shape[1]
    at = lax.broadcasted_iota(jnp.int32, row.shape, 1)
    return jnp.where(at == n - 1, 0.0, pltpu.roll(row, n - 1, 1))


def row_prev(row):
    at = lax.broadcasted_iota(jnp.int32, row.shape, 1)
    return jnp.where(at == 0, 0.0, pltpu.roll(row, 1, 1))


def is_even(axis):
    return lax.rem(lax.axis_index(axis), 2) == 0


class Either:
    def __init__(self, choose, first, second):
        self.choose, self.first, self.second = choose, first, second

    def __getitem__(self, at):
        return jnp.where(self.choose, self.first[at], self.second[at])


def halo_views(near, far):
    even = is_even("tile")
    return Either(even, far, near), Either(even, near, far)


def upward(last, y_above):
    x, y, z = last
    return row_next(y) - y + x, z + (y_above - y)


def fixed_first(field, weight, low, z, zz):
    w = weight[z, 0:1, :]
    return field[0, zz, 0:1, :] + w * low[z, 0:1, :], field[2, zz, 0:1, :] + w * low[z, 1:2, :]


def fixed_last(field, weight, high, z, zz, ny):
    end = slice(ny - 1, ny)
    w = weight[z, end, :]
    hx, hz = high[z, 0:1, :], high[z, 1:2, :]
    rise = hz - high[z - 1, 1:2, :] if z else hz
    return (
        field[0, zz, end, :] + w * hx,
        field[1, zz, end, :] - w * (rise + (hx - row_prev(hx))),
        field[2, zz, end, :] + w * hz,
    )


def lane_masks():
    lane = lax.broadcasted_iota(jnp.int32, (SUB, LANE), 1)
    sub = lax.broadcasted_iota(jnp.int32, (SUB, LANE), 0)
    return lane == 0, lane == LANE - 1, sub == 0, sub == SUB - 1


def tile_at(i, c):
    return slice(i * SUB, (i + 1) * SUB), slice(c * LANE, (c + 1) * LANE)


def pack_kernel(dims, electric, faces, aux, far, block, top, aux_block, sem):
    nz, ny, _ = dims
    even = is_even("tile")
    start = pl.multiple_of(jnp.where(even, 0, ny - SUB), SUB)
    copies = [
        pltpu.make_async_copy(electric.at[:, :, pl.ds(start, SUB)], block, sem.at[0]),
        pltpu.make_async_copy(faces.at[0, 1, 1, pl.ds(ny - SUB, SUB)], top, sem.at[1]),
        pltpu.make_async_copy(aux.at[0, :, :, :, pl.ds(start, SUB)], aux_block, sem.at[2]),
    ]
    for copy in copies:
        copy.start()
    for copy in copies:
        copy.wait()
    end = slice(SUB - 1, SUB)
    for z in range(nz):
        y_above = block[1, z + 1, end, :] if z + 1 < nz else top[end, :]
        up = upward([block[k, z, end, :] for k in range(3)], y_above)
        for q in range(2):
            far[z, q : q + 1, :] = jnp.where(even, block[2 * q, z, 0:1, :], up[q])
    for side in range(2):
        for j in range(TERMS):
            for k in range(2):
                far[nz + side * TERMS + j, k : k + 1, :] = jnp.where(
                    even, aux_block[side, j, k, 0:1, :], aux_block[side, j, k, end, :]
                )


def sweep_plane(load, above, current, weight, store, hx_s, hy_s, dims, from_mass):
    _, ny, nx = dims
    rows, cols = ny // SUB, nx // LANE
    is_first_lane, is_last_lane, is_first_sub, is_last_sub = lane_masks()

    def left(k, i, c):
        return pltpu.roll(load(k, i, c), LANE - 1, 1)

    lefts = {(k, i): left(k, i, 0) for k in (1, 2) for i in range(rows)}
    right_y, right_z = {}, {}
    for c in range(cols):
        here = [[load(k, i, c) for k in range(3)] for i in range(rows)]
        ups = [{k: pltpu.roll(here[i][k], SUB - 1, 0) for k in (0, 2)} for i in range(rows)]
        down_x = down_z = None
        for i in range(rows):
            r, s = tile_at(i, c)

            def y_next(k):
                return jnp.where(is_last_sub, ups[i + 1][k] if i + 1 < rows else 0.0, ups[i][k])

            def x_next(k):
                after = left(k, i, c + 1) if c + 1 < cols else 0.0
                value = jnp.where(is_last_lane, after, lefts[k, i])
                lefts[k, i] = after
                return value

            ex, ey, ez = here[i]
            hx = (y_next(2) - ez) - (above(1, i, c) - ey)
            hy = (above(0, i, c) - ex) - (x_next(2) - ez)
            hz = (x_next(1) - ey) - (y_next(0) - ex)
            hx_low, hy_low = hx_s[r, s], hy_s[r, s]
            hx_s[r, s] = hx
            hy_s[r, s] = hy
            dx = pltpu.roll(hx, 1, 0)
            dz = pltpu.roll(hz, 1, 0)
            hx_y = jnp.where(is_first_sub, ez if i == 0 else down_x, dx)
            hz_y = jnp.where(is_first_sub, -ex if i == 0 else down_z, dz)
            down_x, down_z = dx, dz
            ry = pltpu.roll(hy, 1, 1)
            rz = pltpu.roll(hz, 1, 1)
            hy_x = jnp.where(is_first_lane, 0.0 if c == 0 else right_y[i], ry)
            hz_x = jnp.where(is_first_lane, 0.0 if c == 0 else right_z[i], rz)
            right_y[i], right_z[i] = ry, rz
            cx = (hz - hz_y) - (hy - hy_low)
            cy = (hx - hx_low) - (hz - hz_x)
            cz = (hy - hy_x) - (hx - hx_y)
            w = weight[r, s]
            if from_mass:
                w = 0.5 / (w + 4.0)
                weight[r, s] = w
            keep = 4.0 * w + 0.5
            store(0, i, c, keep * ex + w * (current(0, i, c) - cx))
            store(1, i, c, keep * ey + w * (current(1, i, c) - cy))
            store(2, i, c, keep * ez + w * (current(2, i, c) - cz))


def reader(ref, z):
    def load(k, i, c):
        r, s = tile_at(i, c)
        return ref[k, z, r, s]

    return load


def writer(ref, z):
    def store(k, i, c, value):
        r, s = tile_at(i, c)
        ref[k, z, r, s] = value

    return store


def ghost_flux(load, ghost, hx_s, hy_s, dims):
    _, ny, nx = dims
    for i in range(ny // SUB):
        for c in range(nx // LANE):
            r, s = tile_at(i, c)
            hx_s[r, s] = ghost[1, r, s] - load(1, i, c)
            hy_s[r, s] = load(0, i, c) - ghost[0, r, s]


def first_lower_kernel(
    dims, electric, current_h, mass, faces, aux_h,
    field, current, weight, ghost, flux, near,
    block, top, aux_block, field_sem, current_sem, weight_sem, sem,
):
    nz, ny, _ = dims
    half = nz // 2
    even = is_even("tile")
    end = slice(ny - 1, ny)
    tile_end = slice(SUB - 1, SUB)
    copy = pltpu.make_async_copy
    row = pl.multiple_of(jnp.where(even, ny - SUB, 0), SUB)

    def field_copy(z):
        return copy(electric.at[:, pl.ds(z, 1)], field.at[:, pl.ds(z, 1)], field_sem.at[z])

    def current_copy(z):
        return copy(current_h.at[:, pl.ds(z, 1)], current.at[:, pl.ds(z, 1)], current_sem.at[z])

    def weight_copy(z):
        return copy(mass.at[pl.ds(z, 1)], weight.at[pl.ds(z, 1)], weight_sem.at[z])

    low_copy = copy(faces.at[0, 0], ghost, sem.at[0])
    edge_copies = [
        copy(electric.at[:, pl.ds(half, nz - half), pl.ds(row, SUB)], block, sem.at[1]),
        copy(faces.at[0, 1, 1, pl.ds(ny - SUB, SUB)], top, sem.at[2]),
        copy(aux_h.at[0, :, :, :, pl.ds(row, SUB)], aux_block, sem.at[3]),
    ]
    low_copy.start()
    field_copy(0).start()

    def start(z, carry):
        field_copy(z + 1).start()
        current_copy(z).start()
        weight_copy(z).start()
        return carry

    lax.fori_loop(0, half, start, 0)
    for edge in edge_copies:
        edge.start()

    low_copy.wait()
    field_copy(0).wait()
    hx_s, hy_s = flux.at[0], flux.at[1]
    ghost_flux(reader(field, 0), ghost, hx_s, hy_s, dims)

    def plane(z, carry):
        field_copy(z + 1).wait()
        up = upward([field[k, z, end, :] for k in range(3)], field[1, z + 1, end, :])
        for q in range(2):
            near[z, q : q + 1, :] = jnp.where(even, up[q], field[2 * q, z, 0:1, :])
        current_copy(z).wait()
        weight_copy(z).wait()
        sweep_plane(
            reader(field, z), reader(field, z + 1), reader(current, z), weight.at[z], writer(field, z), hx_s, hy_s, dims, True
        )
        return carry

    lax.fori_loop(0, half, plane, 0)
    for edge in edge_copies:
        edge.wait()
    for z in range(nz - half):
        y_above = block[1, z + 1, tile_end, :] if z + 1 < nz - half else top[tile_end, :]
        up = upward([block[k, z, tile_end, :] for k in range(3)], y_above)
        for q in range(2):
            near[half + z, q : q + 1, :] = jnp.where(even, up[q], block[2 * q, z, 0:1, :])
    for side in range(2):
        for j in range(TERMS):
            for k in range(2):
                near[nz + side * TERMS + j, k : k + 1, :] = jnp.where(
                    even, aux_block[side, j, k, tile_end, :], aux_block[side, j, k, 0:1, :]
                )


def first_upper_kernel(
    dims, electric, current_h, mass, faces, flux,
    field, current, weight,
    flux_s, field_sem, current_sem, weight_sem, sem,
):
    nz, _, _ = dims
    half = nz // 2
    count = nz - half
    copy = pltpu.make_async_copy

    def field_copy(z):
        return copy(electric.at[:, pl.ds(z + half, 1)], field.at[:, pl.ds(z, 1)], field_sem.at[z])

    def current_copy(z):
        return copy(current_h.at[:, pl.ds(z + half, 1)], current.at[:, pl.ds(z, 1)], current_sem.at[z])

    def weight_copy(z):
        return copy(mass.at[pl.ds(z + half, 1)], weight.at[pl.ds(z, 1)], weight_sem.at[z])

    high_copies = [copy(faces.at[0, 1, k], field.at[k, count], sem.at[k]) for k in range(2)]
    field_copy(0).start()

    def start(z, carry):
        field_copy(z + 1).start()
        current_copy(z).start()
        weight_copy(z).start()
        return carry

    lax.fori_loop(0, count - 1, start, 0)
    current_copy(count - 1).start()
    weight_copy(count - 1).start()
    for high in high_copies:
        high.start()
    flux_s[...] = flux[...]
    field_copy(0).wait()

    def plane(z, carry):
        @pl.when(z + 1 < count)
        def _():
            field_copy(z + 1).wait()

        @pl.when(z + 1 == count)
        def _():
            for high in high_copies:
                high.wait()

        current_copy(z).wait()
        weight_copy(z).wait()
        sweep_plane(
            reader(field, z), reader(field, z + 1), reader(current, z),
            weight.at[z], writer(field, z), flux_s.at[0], flux_s.at[1], dims, True,
        )
        return carry

    lax.fori_loop(0, count, plane, 0)


class Planes:
    def __init__(self, lower, upper, half, dim):
        self.lower, self.upper, self.half, self.dim = lower, upper, half, dim

    def __getitem__(self, at):
        z = at[self.dim]
        if z < self.half:
            return self.lower[at]
        return self.upper[at[: self.dim] + (z - self.half,) + at[self.dim + 1 :]]


def fix_rows(dims, fields, ghost, halo, from_below, head, tail, send):
    nz, ny, nx = dims
    half = nz // 2
    end = slice(ny - 1, ny)
    field, current = (Planes(lower, upper, half, 1) for lower, upper in fields[:2])
    weight = Planes(*fields[2], half, 0)

    def value(k, z, r):
        at = slice(r, r + 1)
        if r in (-1, ny) or (k == 2 and z in (-1, nz)):
            return jnp.zeros((1, nx), F32)
        if z == -1:
            return ghost[k, at, :]
        if r == 0 and k != 1:
            return head[z, k // 2 : k // 2 + 1, :]
        if r == ny - 1:
            return tail[z, k : k + 1, :]
        return field[k, z, at, :]

    def flux_x(z, r):
        return (value(2, z, r + 1) - value(2, z, r)) - (value(1, z + 1, r) - value(1, z, r))

    def flux_y(z, r):
        here = value(2, z, r)
        return (value(0, z + 1, r) - value(0, z, r)) - (row_next(here) - here)

    def flux_z(z, r):
        here = value(1, z, r)
        return (row_next(here) - here) - (value(0, z, r + 1) - value(0, z, r))

    def trace(z, r):
        at = slice(r, r + 1)
        hz = flux_z(z, r)
        cx = (hz - flux_z(z, r - 1)) - (flux_y(z, r) - flux_y(z - 1, r))
        cy = (flux_x(z, r) - flux_x(z - 1, r)) - (hz - row_prev(hz))
        w = weight[z, at, :]
        keep = 4.0 * w + 0.5
        return (
            keep * value(0, z, r) + w * (current[0, z, at, :] - cx),
            keep * value(1, z, r) + w * (current[1, z, at, :] - cy),
            w,
        )

    def pack_traces(r):
        for side in range(2):
            x, y, w = trace((nz - 1) * side, r)
            send[nz + side, 0:1, :] = x
            send[nz + side, 1:2, :] = y
            send[nz + 2, side : side + 1, :] = w

    @pl.when(from_below)
    def _():
        for z in range(nz):
            x, zc = fixed_first(field, weight, halo, z, z)
            head[z, 0:1, :], head[z, 1:2, :] = x, zc
            send[z, 0:1, :], send[z, 1:2, :] = x, zc
        head[nz, 0:1, :] = field[0, nz, 0:1, :]
        pack_traces(0)

    @pl.when(jnp.logical_not(from_below))
    def _():
        for z in range(nz):
            x, y, zc = fixed_last(field, weight, halo, z, z, ny)
            tail[z, 0:1, :], tail[z, 1:2, :], tail[z, 2:3, :] = x, y, zc
        tail[nz, 0:1, :] = field[0, nz, end, :]
        tail[nz, 1:2, :] = field[1, nz, end, :]
        for z in range(nz):
            up = upward([tail[z, k : k + 1, :] for k in range(3)], tail[z + 1, 1:2, :])
            send[z, 0:1, :], send[z, 1:2, :] = up
        pack_traces(ny - 1)


def fix_far_kernel(
    dims, field_a, field_b, current_a, current_b, weight_a, weight_b, ghost, far, head, tail, send
):
    fields = ((field_a, field_b), (current_a, current_b), (weight_a, weight_b))
    fix_rows(dims, fields, ghost, far, is_even("tile"), head, tail, send)


def fix_near_kernel(
    dims, field_a, field_b, current_a, current_b, weight_a, weight_b, ghost, near, head_f, tail_f,
    head, tail, send,
):
    even = is_even("tile")
    fields = ((field_a, field_b), (current_a, current_b), (weight_a, weight_b))

    @pl.when(even)
    def _():
        head[...] = head_f[...]

    @pl.when(jnp.logical_not(even))
    def _():
        tail[...] = tail_f[...]

    fix_rows(dims, fields, ghost, near, jnp.logical_not(even), head, tail, send)


def edged_reader(ref, z, head, tail, plane, ny):
    rows = ny // SUB
    _, _, is_first_sub, is_last_sub = lane_masks()

    def load(k, i, c):
        r, s = tile_at(i, c)
        value = ref[k, z, r, s]
        if i == 0 and k != 1:
            value = jnp.where(is_first_sub, head[plane, k // 2 : k // 2 + 1, s], value)
        if i == rows - 1:
            value = jnp.where(is_last_sub, tail[plane, k : k + 1, s], value)
        return value

    return load


def second_lower_kernel(
    dims, old_a, old_b, current, weight, ghost, head, tail, near_rows, field, flux, near_next
):
    nz, ny, _ = dims
    half = nz // 2
    near_next[...] = near_rows[...]
    hx_s, hy_s = flux.at[0], flux.at[1]
    ghost_flux(edged_reader(old_a, 0, head, tail, 0, ny), ghost, hx_s, hy_s, dims)

    def sweep(z, above):
        sweep_plane(
            edged_reader(old_a, z, head, tail, z, ny), above, reader(current, z), weight.at[z],
            writer(field, z), hx_s, hy_s, dims, False,
        )

    def plane(z, carry):
        sweep(z, edged_reader(old_a, z + 1, head, tail, z + 1, ny))
        return carry

    lax.fori_loop(0, half - 1, plane, 0)
    sweep(half - 1, edged_reader(old_b, 0, head, tail, half, ny))


def inner_copies(field, smoothed, sem, start, z, count, ny):
    inner = pl.ds(SUB, ny - 2 * SUB)
    return pltpu.make_async_copy(
        field.at[:, pl.ds(z, count), inner], smoothed.at[:, pl.ds(start + z, count), inner], sem
    )


LATE = 2


def second_upper_kernel(
    dims, old, current, weight, flux, head, tail, lower, aux_h, field, smoothed, aux, flux_s, sem
):
    nz, ny, _ = dims
    half = nz // 2
    count = nz - half
    early = inner_copies(lower, smoothed, sem.at[count], 0, 0, half, ny)
    early.start()
    load = pltpu.make_async_copy(aux_h.at[0], aux, sem.at[count + 1])
    load.start()
    flux_s[...] = flux[...]

    def out(z):
        return inner_copies(field, smoothed, sem.at[z], half, z, 1, ny)

    def plane(z, carry):
        at = z + half
        sweep_plane(
            edged_reader(old, z, head, tail, at, ny), edged_reader(old, z + 1, head, tail, at + 1, ny),
            reader(current, z), weight.at[z], writer(field, z), flux_s.at[0], flux_s.at[1], dims, False,
        )

        @pl.when(z < count - LATE)
        def _():
            out(z).start()

        return carry

    lax.fori_loop(0, count, plane, 0)
    for z in range(count - LATE):
        out(z).wait()
    early.wait()
    load.wait()


def fix_trace_kernel(
    dims, field_a, field_b, weight_a, weight_b, near1, far1, head1, tail1, near, far,
    head, tail, traces, below, above,
):
    nz, ny, _ = dims
    half = nz // 2
    end = slice(ny - 1, ny)
    field = Planes(field_a, field_b, half, 1)
    weight = Planes(weight_a, weight_b, half, 0)
    low, high = halo_views(near, far)
    low1, high1 = halo_views(near1, far1)
    for side in range(2):
        z = (nz - 1) * side
        for k in range(2):
            traces[side, k] = field[k, z]
    for z in range(nz):
        head[z, 0:1, :], head[z, 1:2, :] = fixed_first(field, weight, low, z, z)
        x, y, zc = fixed_last(field, weight, high, z, z, ny)
        tail[z, 0:1, :], tail[z, 1:2, :], tail[z, 2:3, :] = x, y, zc
        if z in (0, nz - 1):
            side = 0 if z == 0 else 1
            traces[side, 0, 0:1, :] = head[z, 0:1, :]
            traces[side, 0, end, :] = x
            traces[side, 1, end, :] = y
    for side in range(2):
        z = (nz - 1) * side
        x, zc = head1[z, 0:1, :], head1[z, 1:2, :]
        rise = zc - head1[z - 1, 1:2, :] if z else zc
        w = low[nz + 2, side : side + 1, :]
        trace_low = (
            low[nz + side, 0:1, :] + w * x,
            low[nz + side, 1:2, :] - w * (rise + (x - row_prev(x))),
        )
        y = tail1[z, 1:2, :]
        w = high[nz + 2, side : side + 1, :]
        trace_high = (
            high[nz + side, 0:1, :] + w * (row_next(y) - y + tail1[z, 0:1, :]),
            high[nz + side, 1:2, :],
        )
        for k in range(2):
            for j in range(TERMS):
                at = side * TERMS + j
                below[at, k : k + 1, :] = trace_low[k] - pade_decays[j] * low1[nz + at, k : k + 1, :]
                above[at, k : k + 1, :] = trace_high[k] - pade_decays[j] * high1[nz + at, k : k + 1, :]


def surface_tiles(dims, k, value, edge_low, edge_high, emit):
    _, ny, nx = dims
    rows, cols = ny // SUB, nx // LANE
    is_first_lane, is_last_lane, is_first_sub, is_last_sub = lane_masks()
    column = [value(i, 0) for i in range(rows)]
    lefts = [pltpu.roll(u, LANE - 1, 1) for u in column]
    rights = [0.0] * rows
    for c in range(cols):
        s = slice(c * LANE, (c + 1) * LANE)
        ups = [pltpu.roll(u, SUB - 1, 0) for u in column] + [edge_high(s)]
        downs = [edge_low(s)] + [pltpu.roll(u, 1, 0) for u in column]
        after = [value(i, c + 1) for i in range(rows)] if c + 1 < cols else None
        for i in range(rows):
            u = column[i]
            y_next = jnp.where(is_last_sub, ups[i + 1], ups[i])
            y_prev = jnp.where(is_first_sub, downs[i], downs[i + 1])
            if after is not None:
                beyond = pltpu.roll(after[i], LANE - 1, 1)
            else:
                beyond = u if k == 0 else 0.0
            x_next = jnp.where(is_last_lane, beyond, lefts[i])
            lefts[i] = beyond
            right = pltpu.roll(u, 1, 1)
            before = rights[i] if c else (u if k == 1 else 0.0)
            x_prev = jnp.where(is_first_lane, before, right)
            rights[i] = right
            emit(i, c, 0.5 * u - 0.125 * ((y_next + y_prev) + (x_next + x_prev)))
        column = after


def outgoing_kernel(dims, traces, aux, below, above, even_side, odd_side):
    even = is_even("slab")
    total = sum(pade_weights)
    for out, side in ((even_side, jnp.where(even, 1, 0)), (odd_side, jnp.where(even, 0, 1))):
        for k in range(2):

            def value(i, c):
                r, s = tile_at(i, c)
                u = total * traces[side, k, r, s]
                for j in range(TERMS):
                    u = u - (pade_weights[j] * pade_decays[j]) * aux[side, j, k, r, s]
                return u

            def edge(source):
                def row(s):
                    u = 0.0
                    for j in range(TERMS):
                        u = u + pade_weights[j] * source[side * TERMS + j, k : k + 1, s]
                    return u

                return row

            def emit(i, c, new):
                r, s = tile_at(i, c)
                out[k, r, s] = traces[side, k, r, s] + new

            surface_tiles(dims, k, value, edge(below), edge(above), emit)


def surface_kernel(dims, traces, aux, below, above, out, fresh, sem):
    def copy(side, j):
        return pltpu.make_async_copy(fresh.at[side, j], out.at[0, side, j], sem.at[side * TERMS + j])

    def term(at, carry):
        side, j = at // TERMS, at % TERMS
        decay = F32(0.0)
        for q in range(TERMS):
            decay = jnp.where(j == q, F32(pade_decays[q]), decay)
        for k in range(2):

            def value(i, c):
                r, s = tile_at(i, c)
                return traces[side, k, r, s] - decay * aux[side, j, k, r, s]

            def emit(i, c, new):
                r, s = tile_at(i, c)
                fresh[side, j, k, r, s] = new

            surface_tiles(
                dims, k, value, lambda s: below[at, k : k + 1, s], lambda s: above[at, k : k + 1, s], emit
            )
        copy(side, j).start()
        return carry

    lax.fori_loop(0, 2 * TERMS, term, 0)
    for side in range(2):
        for j in range(TERMS):
            copy(side, j).wait()


def write_kernel(dims, field_a, field_b, head, tail, old, smoothed, edges, sem):
    nz, ny, nx = dims
    half = nz // 2
    count = nz - half
    _, _, is_first_sub, is_last_sub = lane_masks()
    copies = [inner_copies(field_b, smoothed, sem.at[0], half, count - LATE, LATE, ny)]
    copies[0].start()
    for n, (field, start, planes) in enumerate(((field_a, 0, half), (field_b, half, count))):

        def merge(z, carry):
            at = z + start
            for c in range(nx // LANE):
                s = slice(c * LANE, (c + 1) * LANE)
                for k in range(3):
                    value = field[k, z, 0:SUB, s]
                    if k != 1:
                        value = jnp.where(is_first_sub, head[at, k // 2 : k // 2 + 1, s], value)
                    edges[0, k, at, :, s] = value
                    value = field[k, z, ny - SUB : ny, s]
                    edges[1, k, at, :, s] = jnp.where(is_last_sub, tail[at, k : k + 1, s], value)
            return carry

        lax.fori_loop(0, planes, merge, 0)
        span = pl.ds(start, planes)
        for e, row in enumerate((0, ny - SUB)):
            copies.append(
                pltpu.make_async_copy(
                    edges.at[e, :, span], smoothed.at[:, span, pl.ds(row, SUB)], sem.at[1 + 2 * n + e]
                )
            )
            copies[-1].start()
    for copy in copies:
        copy.wait()


def faces_kernel(even_side, odd_side, out, sem):
    below = jnp.where(is_even("slab"), 0, 1)
    copies = [
        pltpu.make_async_copy(odd_side, out.at[0, below], sem.at[0]),
        pltpu.make_async_copy(even_side, out.at[0, 1 - below], sem.at[1]),
    ]
    for copy in copies:
        copy.start()
    for copy in copies:
        copy.wait()


def call(kernel, **options):
    return pl.pallas_call(kernel, **options)


def swap(block, axis, first):
    pairs = [(i, i + 1) for i in range(first, lax.axis_size(axis) - 1, 2)]
    return lax.ppermute(block, axis, [p for i, j in pairs for p in ((i, j), (j, i))])


def iteration(electric, current, mass, faces, aux):
    nz, ny, nx = mass.shape
    half = nz // 2
    dims = (nz, ny, nx)
    cells = nz * ny * nx
    bind = functools.partial
    rows1, rows2 = shape(nz + 2 * TERMS, 2, nx), shape(nz + 3, 2, nx)
    flux_shape = shape(2, ny, nx)
    dma = pltpu.SemaphoreType.DMA
    electric, current, mass, faces, aux = (
        pltpu.with_memory_space_constraint(a, pltpu.HBM) for a in (electric, current, mass, faces, aux)
    )
    aux_block = vm(2, TERMS, 2, SUB, nx)
    count = nz - half

    far1 = call(
        bind(pack_kernel, dims),
        out_shape=rows1,
        in_specs=[HBM] * 3,
        out_specs=VM,
        scratch_shapes=[vm(3, nz, SUB, nx), vm(SUB, nx), aux_block, dma((3,))],
        compiler_params=params(12),
    )(electric, faces, aux)
    far1 = swap(far1, "tile", 1)

    lower, current_a, weight_a, ghost, flux, near1 = call(
        bind(first_lower_kernel, dims),
        out_shape=(
            shape(3, half + 1, ny, nx),
            shape(3, half, ny, nx),
            shape(half, ny, nx),
            flux_shape,
            flux_shape,
            rows1,
        ),
        in_specs=[HBM] * 5,
        out_specs=(VM,) * 6,
        scratch_shapes=[vm(3, count, SUB, nx), vm(SUB, nx), aux_block]
        + [dma((half + 1,)), dma((half,)), dma((half,)), dma((4,))],
        compiler_params=params(16),
        cost_estimate=cost(25 * cells, 14 * cells),
    )(electric, current, mass, faces, aux)
    near1 = swap(near1, "tile", 0)

    upper, current_b, weight_b = call(
        bind(first_upper_kernel, dims),
        out_shape=(
            shape(3, count + 1, ny, nx),
            shape(3, count, ny, nx),
            shape(count, ny, nx),
        ),
        in_specs=[HBM] * 4 + [VM],
        out_specs=(VM,) * 3,
        scratch_shapes=[vm(2, ny, nx), dma((count,)), dma((count,)), dma((count,)), dma((2,))],
        compiler_params=params(16),
        cost_estimate=cost(25 * cells, 14 * cells),
    )(electric, current, mass, faces, flux)

    heads, tails = shape(nz + 1, 2, nx), shape(nz + 1, 3, nx)
    state = (lower, upper, current_a, current_b, weight_a, weight_b, ghost)
    head_f, tail_f, far2 = call(
        bind(fix_far_kernel, dims),
        out_shape=(heads, tails, rows2),
        in_specs=[VM] * 8,
        out_specs=(VM,) * 3,
        compiler_params=params(8),
    )(*state, far1)
    far2 = swap(far2, "tile", 1)
    head1, tail1, near_rows = call(
        bind(fix_near_kernel, dims),
        out_shape=(heads, tails, rows2),
        in_specs=[VM] * 10,
        out_specs=(VM,) * 3,
        compiler_params=params(8),
    )(*state, near1, head_f, tail_f)

    lower2, flux, near2 = call(
        bind(second_lower_kernel, dims),
        out_shape=(shape(3, half, ny, nx), flux_shape, rows2),
        in_specs=[VM] * 8,
        out_specs=(VM,) * 3,
        compiler_params=params(12),
        cost_estimate=cost(20 * cells, 14 * cells),
    )(lower, upper, current_a, weight_a, ghost, head1, tail1, near_rows)
    near2 = swap(near2, "tile", 0)

    upper2, smoothed, aux_v = call(
        bind(second_upper_kernel, dims),
        out_shape=(shape(3, count, ny, nx), shape(3, nz, ny, nx), shape(2, TERMS, 2, ny, nx)),
        in_specs=[VM] * 7 + [HBM],
        out_specs=(VM, HBM, VM),
        scratch_shapes=[vm(2, ny, nx), dma((count + 2,))],
        compiler_params=params(12),
        cost_estimate=cost(20 * cells, 14 * cells),
    )(upper, current_b, weight_b, flux, head1, tail1, lower2, aux)

    edge_rows = shape(2 * TERMS, 2, nx)
    head, tail, traces, below, above = call(
        bind(fix_trace_kernel, dims),
        out_shape=(heads, tails, shape(2, 2, ny, nx), edge_rows, edge_rows),
        in_specs=[VM] * 10,
        out_specs=(VM,) * 5,
        compiler_params=params(12),
    )(lower2, upper2, weight_a, weight_b, near1, far1, head1, tail1, near2, far2)

    even_side, odd_side = call(
        bind(outgoing_kernel, dims),
        out_shape=(flux_shape, flux_shape),
        in_specs=[VM] * 4,
        out_specs=(VM,) * 2,
        compiler_params=params(8),
    )(traces, aux_v, below, above)
    odd_side = swap(odd_side, "slab", 1)
    even_side = swap(even_side, "slab", 0)

    fresh = call(
        bind(surface_kernel, dims),
        out_shape=shape(1, 2, TERMS, 2, ny, nx),
        in_specs=[VM] * 4,
        out_specs=HBM,
        scratch_shapes=[vm(2, TERMS, 2, ny, nx), dma((2 * TERMS,))],
        compiler_params=params(8),
        cost_estimate=cost(12 * 16 * ny * nx, 12 * 16 * ny * nx),
    )(traces, aux_v, below, above)

    smoothed = call(
        bind(write_kernel, dims),
        out_shape=shape(3, nz, ny, nx),
        in_specs=[VM] * 4 + [HBM],
        out_specs=HBM,
        input_output_aliases={4: 0},
        scratch_shapes=[vm(2, 3, nz, SUB, nx), dma((5,))],
        compiler_params=params(12),
        cost_estimate=cost(cells, 12 * cells),
    )(lower2, upper2, head, tail, smoothed)

    next_faces = call(
        faces_kernel,
        out_shape=shape(1, 2, 2, ny, nx),
        in_specs=[VM] * 2,
        out_specs=HBM,
        scratch_shapes=[dma((2,))],
        compiler_params=params(8),
    )(even_side, odd_side)
    return smoothed, next_faces, fresh


def solution(mesh):
    placed = (
        P(None, "slab", "tile", None),
        P(None, "slab", "tile", None),
        P("slab", "tile", None),
        P("slab", None, None, "tile", None),
        P("slab", None, None, None, "tile", None),
    )
    return jax.shard_map(
        iteration,
        mesh=mesh,
        in_specs=placed,
        out_specs=(
            P(None, "slab", "tile", None),
            P("slab", None, None, "tile", None),
            P("slab", None, None, None, "tile", None),
        ),
        check_vma=False,
    )
```
